128 devices in a mesh: ctx: 32 (over x, y, core), head: 4 (over z).
Axes of the slice: x: 4, y: 4, z: 4, core: 2. Of those that a mesh axis runs over, the one named last changes fastest.
Arguments:
- tokens: bfloat16 [8192, 2048], P('ctx'), may hold values from -6 to 6
- qkv_weight: bfloat16 [2048, 3, 16, 128], P(None, None, 'head'), may hold values from -0.125 to 0.125
- small_weight: bfloat16 [2048, 16, 15], P(None, 'head'), may hold values from -0.125 to 0.125
- head_param: float32 [16, 2], P('head'), as said below
- norm_gain: float32 [128], replicated, may hold values from 0.1 to 1.9
- out_weight: bfloat16 [16, 128, 2048], P('head'), may hold values from -0.125 to 0.125
- grad_out: bfloat16 [8192, 2048], P('ctx'), may hold values from -6 to 6
Outputs:
- layer_out: bfloat16 [8192, 2048], P('ctx', 'head')
- grad_tokens: bfloat16 [8192, 2048], P('ctx', 'head')
The draws below stay inside these ranges and needn't reach their ends.
Inputs may be any that keep to these rules, and one draw needn't show every extreme that they name: `head_param`: column 0 holds each head's decay rate, positive; column 1 a bias added before the write strength's sigmoid.
All inputs are finite; a program needn't handle non-finite values.
Results may differ from the reference program's by a relative error of at most 0.017.
Values may be sent and summed in bfloat16 or wider, within the bound.
A program may use at most 128 MiB of HBM per device.

```python
import jax
import jax.numpy as jnp
from jax import lax

D = 2048
H = 16
DK = 128
BLOCK = 64
LV = 13
TOKENS = 8192
NS = 15
N_HEAD = 4


def draw_head_param(key, part):
    key_rate, key_bias = jax.random.split(jax.random.fold_in(key, 7))
    slow_end = jnp.log(0.5 / TOKENS)
    fast_end = jnp.log(0.05)
    share_pos = jax.random.uniform(key_rate, (H,), jnp.float32)
    decay_rate = jnp.exp(slow_end + share_pos * (fast_end - slow_end))
    write_bias = jnp.log(64.0 * decay_rate) + jax.random.uniform(key_bias, (H,), jnp.float32, -0.5, 0.5)
    return jnp.stack([decay_rate, write_bias], 1)


def steps_of(key, extent, cuts, smallest, top_value):
    gain, own = 1.0, jax.random.fold_in(key, 6)
    for dim, parts in cuts:
        heights = jnp.exp(jax.random.uniform(jax.random.fold_in(own, dim), (parts,), jnp.float32, smallest / len(cuts), top_value / len(cuts)))
        gain = gain * jnp.repeat(heights, extent[dim] // parts).reshape([-1 if axis == dim else 1 for axis in range(len(extent))])
    return gain


def gaussian(key, extent, scale, bound, cuts=(), kind=jnp.bfloat16):
    factor_of = steps_of(key, extent, cuts, -0.22, 0.18) if cuts else 1.0
    array = jax.random.normal(key, extent, jnp.float32) * scale * factor_of
    return jnp.minimum(jnp.maximum(array, -bound), bound).astype(kind)


def setup_inputs(seed: int = 0) -> dict:
    key_of = jax.random.split(jax.random.key(seed), 8)
    return {
        "tokens": gaussian(key_of[0], (TOKENS, D), 1.0, 6.0, ((0, 32),)),
        "qkv_weight": gaussian(key_of[1], (D, 3, H, DK), D ** -0.5, 0.125, ((2, 4),)),
        "small_weight": gaussian(key_of[2], (D, H, NS), D ** -0.5, 0.125, ((1, 4),)),
        "head_param": draw_head_param(jax.random.fold_in(key_of[7], 71), 0),
        "norm_gain": jnp.clip(1.0 + 0.18 * jax.random.normal(key_of[4], (DK,), jnp.float32), 0.1, 1.9),
        "out_weight": gaussian(key_of[5], (H, DK, D), (H * DK) ** -0.5, 0.125, ((0, 4),)),
        "grad_out": gaussian(key_of[6], (TOKENS, D), 1.0, 6.0, ((0, 32),)),
    }


def mat_mul(left, right):
    return jnp.matmul(left, right, precision=lax.Precision.HIGHEST)

def flip_last(array_in):
    return jnp.swapaxes(array_in, -1, -2)

def unit_scale(values):
    return values * lax.rsqrt(lax.optimization_barrier(jnp.sum(values * values, -1, keepdims=True)) + 1e-06)

def block_pieces(q_in, k_in, v_in, beta_w, decay_log):
    length = q_in.shape[-2]
    cum_log = jnp.cumsum(decay_log, axis=-1)
    row_id = lax.broadcasted_iota(jnp.int32, (length, length), 0)
    col_id = lax.broadcasted_iota(jnp.int32, (length, length), 1)
    inclusive = row_id >= col_id
    strict = row_id > col_id
    spread = cum_log[..., :, None] - cum_log[..., None, :]
    decay_mat = jnp.where(inclusive, jnp.exp(jnp.where(inclusive, spread, 0.0)), 0.0)
    key_gram = mat_mul(k_in, flip_last(k_in))
    lower_part = jnp.where(strict, beta_w[..., :, None] * decay_mat * key_gram, 0.0)
    system = lower_part + jnp.eye(length, dtype=jnp.float32)
    growth = jnp.exp(cum_log)
    right_side = jnp.concatenate([beta_w[..., None] * v_in, (beta_w * growth)[..., None] * k_in], -1)
    solved = jax.scipy.linalg.solve_triangular(system, right_side, lower=True, unit_diagonal=True)
    value_dim = v_in.shape[-1]
    new_values = solved[..., :value_dim]
    key_mix = solved[..., value_dim:]
    scores = mat_mul(q_in, flip_last(k_in)) * decay_mat
    intra_out = mat_mul(scores, new_values)
    query_mix = growth[..., None] * q_in - mat_mul(scores, key_mix)
    tail_decay = jnp.exp(cum_log[..., -1:] - cum_log)
    tail_keys = tail_decay[..., None] * k_in
    eye_key = jnp.eye(k_in.shape[-1], dtype=jnp.float32)
    transit = jnp.exp(cum_log[..., -1])[..., None, None] * eye_key - mat_mul(flip_last(key_mix), tail_keys)
    own_state = mat_mul(flip_last(new_values), tail_keys)
    return (intra_out, query_mix, transit, own_state)

def butterfly(transit, own_state):
    total_count = transit.shape[0]
    eye_key = jnp.eye(transit.shape[-1], dtype=jnp.float32)
    prefix = jnp.broadcast_to(eye_key, transit.shape)
    block_a = transit
    block_u = own_state
    found_all = []
    block_len = 1
    while block_len < total_count:
        pair_count = total_count // (2 * block_len)
        split_a = block_a.reshape((pair_count, 2) + block_a.shape[1:])
        split_u = block_u.reshape((pair_count, 2) + block_u.shape[1:])
        split_p = prefix.reshape((pair_count, 2, block_len) + prefix.shape[1:])
        low_a = split_a[:, 0]
        high_a = split_a[:, 1]
        low_u = split_u[:, 0]
        high_u = split_u[:, 1]
        upper_p = split_p[:, 1]
        arriving = mat_mul(low_u[:, None], upper_p)
        moved_p = mat_mul(low_a[:, None], upper_p)
        found_all.append(jnp.stack([jnp.zeros_like(arriving), arriving], 1).reshape(own_state.shape))
        prefix = jnp.stack([split_p[:, 0], moved_p], 1).reshape(prefix.shape)
        block_a = mat_mul(low_a, high_a)
        block_u = mat_mul(low_u, high_a) + high_u
        block_len = block_len * 2
    return (found_all, prefix, block_a[0], block_u[0])

def head_output(q_raw, k_raw, v_raw, gate_pre, decay_rate, write_bias, norm_gain):
    token_count = q_raw.shape[0]
    block_count = token_count // BLOCK

    def to_blocks(tensor):
        return tensor.reshape((block_count, BLOCK) + tensor.shape[1:])
    beta_w = jax.nn.sigmoid(gate_pre[:, LV + 1] + write_bias)
    decay_log = -decay_rate * jax.nn.sigmoid(gate_pre[:, LV])
    weights = to_blocks(jax.nn.softplus(gate_pre[:, :LV]))
    intra_out, query_mix, transit, own_state = block_pieces(to_blocks(unit_scale(q_raw)), to_blocks(unit_scale(k_raw)), to_blocks(v_raw), to_blocks(beta_w), to_blocks(decay_log))
    found_all, prefix, block_a, block_u = butterfly(transit, own_state)
    summed = weights[..., 0:1] * intra_out
    for level_no in range(len(found_all)):
        summed = summed + weights[..., level_no + 1:level_no + 2] * mat_mul(query_mix, flip_last(found_all[level_no]))
    summed = summed.reshape(token_count, q_raw.shape[1])
    return summed * lax.rsqrt(lax.optimization_barrier(jnp.mean(summed * summed, -1, keepdims=True)) + 1e-06) * norm_gain

def reference(tokens, qkv_weight, small_weight, head_param, norm_gain, out_weight, grad_out):
    token_count = tokens.shape[0]
    proj = jnp.dot(tokens.astype(jnp.float32), qkv_weight.reshape(D, 3 * H * DK).astype(jnp.float32), preferred_element_type=jnp.float32)
    proj = proj.reshape(token_count, 3, H, DK)
    gate_pre = jnp.dot(tokens.astype(jnp.float32), small_weight.reshape(D, H * NS).astype(jnp.float32), preferred_element_type=jnp.float32)
    gate_pre = gate_pre.reshape(token_count, H, NS)

    def one_head(packed):
        return head_output(packed[0], packed[1], packed[2], packed[3], packed[4], packed[5], norm_gain)
    saved_head = jax.checkpoint(one_head)

    def core_all(q_all, k_all, v_all, gate_all):
        return lax.map(saved_head, (q_all, k_all, v_all, gate_all, head_param[:, 0], head_param[:, 1]))
    q_all = jnp.transpose(proj[:, 0], (1, 0, 2))
    k_all = jnp.transpose(proj[:, 1], (1, 0, 2))
    v_all = jnp.transpose(proj[:, 2], (1, 0, 2))
    gate_all = jnp.transpose(gate_pre, (1, 0, 2))
    normed, pull_back = jax.vjp(core_all, q_all, k_all, v_all, gate_all)
    normed_low = jnp.transpose(normed.astype(jnp.bfloat16), (1, 0, 2))
    group_size = H // N_HEAD
    layer_sum = jnp.zeros((token_count, D), jnp.float32)
    for group_no in range(N_HEAD):
        first = group_no * group_size
        partial_value = jnp.dot(normed_low[:, first:first + group_size].reshape(token_count, group_size * DK).astype(jnp.float32), out_weight[first:first + group_size].reshape(group_size * DK, D).astype(jnp.float32), preferred_element_type=jnp.float32)
        layer_sum = layer_sum + lax.optimization_barrier(partial_value.astype(jnp.bfloat16)).astype(jnp.float32)
    grad_normed = jnp.dot(grad_out.astype(jnp.float32), out_weight.reshape(H * DK, D).T.astype(jnp.float32), preferred_element_type=jnp.float32)
    grad_normed = jnp.transpose(grad_normed.reshape(token_count, H, DK), (1, 0, 2))
    grad_q, grad_k, grad_v, grad_gate = pull_back(grad_normed)
    grad_proj = jnp.stack([grad_q, grad_k, grad_v], 0)
    grad_proj = jnp.transpose(grad_proj, (2, 0, 1, 3)).astype(jnp.bfloat16)
    grad_gate = jnp.transpose(grad_gate, (1, 0, 2)).astype(jnp.bfloat16)
    grad_sum = jnp.zeros((token_count, D), jnp.float32)
    for group_no in range(N_HEAD):
        first = group_no * group_size
        partial_value = jnp.dot(grad_proj[:, :, first:first + group_size].reshape(token_count, 3 * group_size * DK).astype(jnp.float32), qkv_weight[:, :, first:first + group_size].reshape(D, 3 * group_size * DK).T.astype(jnp.float32), preferred_element_type=jnp.float32)
        partial_value = partial_value + jnp.dot(grad_gate[:, first:first + group_size].reshape(token_count, group_size * NS).astype(jnp.float32), small_weight[:, first:first + group_size].reshape(D, group_size * NS).T.astype(jnp.float32), preferred_element_type=jnp.float32)
        grad_sum = grad_sum + lax.optimization_barrier(partial_value.astype(jnp.bfloat16)).astype(jnp.float32)
    return (layer_sum.astype(jnp.bfloat16), grad_sum.astype(jnp.bfloat16))
```

```python
import functools

import jax
import jax.numpy as jnp
from jax import lax
from jax.experimental import pallas as pl
from jax.experimental.pallas import tpu as pltpu
from jax.sharding import PartitionSpec as P

BF = jnp.bfloat16
F32 = jnp.float32
LANES = 32
VM = pltpu.VMEM


def nn(a, b):
    return lax.dot_general(a, b, (((1,), (0,)), ((), ())), preferred_element_type=F32)


def nt(a, b):
    return lax.dot_general(a, b, (((1,), (1,)), ((), ())), preferred_element_type=F32)


def tn(a, b):
    return lax.dot_general(a, b, (((0,), (0,)), ((), ())), preferred_element_type=F32)


def sigmoid(x):
    return 1.0 / (1.0 + jnp.exp(-x))


def softplus(x):
    return jnp.maximum(x, 0.0) + jnp.log(1.0 + jnp.exp(-jnp.abs(x)))


def iotas(n, m):
    return lax.broadcasted_iota(jnp.int32, (n, m), 0), lax.broadcasted_iota(jnp.int32, (n, m), 1)


def col(array, lane):
    return array[:, lane : lane + 1]


def head_rows(param_ref, heads, rows):
    lane = lax.broadcasted_iota(jnp.int32, (rows, heads * LANES), 1)
    rate = jnp.zeros((rows, heads * LANES), F32)
    bias = jnp.zeros((rows, heads * LANES), F32)
    for h in range(heads):
        here = lane // LANES == h
        rate = jnp.where(here, param_ref[h, 0], rate)
        bias = jnp.where(here, param_ref[h, 1], bias)
    return rate, bias


def proj_kernel(heads, extra, tok_ref, w_ref, sw_ref, proj_ref, gate_ref, wflat_ref, swflat_ref, wide, swide):
    step = pl.program_id(0)
    parts = 3 * heads
    depth = tok_ref.shape[1]
    wide[...] = w_ref[...].astype(F32)
    swide[...] = sw_ref[...].astype(F32)
    for part in range(parts):
        wflat_ref[:, part * 128 : (part + 1) * 128] = wide[pl.ds(part, depth, stride=parts), :].astype(BF)
    swflat_ref[...] = jnp.zeros_like(swflat_ref)
    for h in range(heads):
        swflat_ref[:, h * LANES : h * LANES + extra] = swide[pl.ds(h, depth, stride=heads), :].astype(BF)

    @pl.when(step == 0)
    def _():
        proj_ref[...] = jnp.zeros_like(proj_ref)
        gate_ref[...] = jnp.zeros_like(gate_ref)

    tok = tok_ref[...]
    proj_ref[...] += nn(tok, wflat_ref[...])
    gate_ref[...] += nn(tok, swflat_ref[...])


def project(tokens, qkv_weight, small_weight):
    rows, width = tokens.shape
    heads = qkv_weight.shape[2]
    extra = small_weight.shape[2]
    parts = 3 * heads
    depth = 256
    return pl.pallas_call(
        functools.partial(proj_kernel, heads, extra),
        grid=(width // depth,),
        in_specs=[
            pl.BlockSpec((rows, depth), lambda i: (0, i)),
            pl.BlockSpec((depth * parts, 128), lambda i: (i, 0)),
            pl.BlockSpec((depth * heads, extra), lambda i: (i, 0)),
        ],
        out_specs=[
            pl.BlockSpec((rows, parts * 128), lambda i: (0, 0)),
            pl.BlockSpec((rows, heads * LANES), lambda i: (0, 0)),
            pl.BlockSpec((depth, parts * 128), lambda i: (i, 0)),
            pl.BlockSpec((depth, heads * LANES), lambda i: (i, 0)),
        ],
        out_shape=[
            jax.ShapeDtypeStruct((rows, parts * 128), F32),
            jax.ShapeDtypeStruct((rows, heads * LANES), F32),
            jax.ShapeDtypeStruct((width, parts * 128), BF),
            jax.ShapeDtypeStruct((width, heads * LANES), BF),
        ],
        scratch_shapes=[VM((depth * parts, 128), F32), VM((depth * heads, extra), F32)],
        name="project",
    )(tokens, qkv_weight.reshape(width * parts, 128), small_weight.reshape(width * heads, extra))


def unit(values):
    scale = lax.rsqrt(jnp.sum(values * values, -1, keepdims=True) + 1e-06)
    return values * scale, scale


def running_log(gate, rate, n):
    row, lane = iotas(n, n)
    lower = jnp.where(row >= lane, 1.0, 0.0).astype(F32)
    return lax.dot_general(
        lower, -rate * sigmoid(gate), (((1,), (0,)), ((), ())),
        precision=lax.Precision.HIGHEST, preferred_element_type=F32,
    )


def mask_rows(n, masks):
    row, lane = iotas(n, n)
    cross = jnp.bitwise_xor(row, lane)
    for k in range(masks.shape[0]):
        masks[k] = jnp.where(jnp.right_shift(cross, k) == 1, 1.0, 0.0).astype(BF)


def local_kernel(heads, levels, group, param_ref, proj_ref, gate_ref, au_ref, e_ref, s_ref, lp_ref, t_ref, m_ref,
                 nk_ref, core_ref, qh_ref, clog_ref, masks, low):
    n = proj_ref.shape[0]
    gate = gate_ref[...]
    rate, bias = head_rows(param_ref, heads, n)
    clog = running_log(gate, rate, n)
    clog_ref[...] = clog
    clog_t = clog.T
    beta_all = sigmoid(gate + bias)
    lam_all = softplus(gate)
    mask_rows(n, masks)
    row, lane = iotas(n, n)
    cross = jnp.bitwise_xor(row, lane)
    incl = row >= lane
    strict = row > lane
    half = n // 2
    for first in range(0, heads, group):
        hs = range(first, first + group)
        keep = {}
        tb = {}
        for h in hs:
            base = h * LANES
            q, _ = unit(proj_ref[:, h * 128 : (h + 1) * 128])
            k, _ = unit(proj_ref[:, (heads + h) * 128 : (heads + h + 1) * 128])
            v = proj_ref[:, (2 * heads + h) * 128 : (2 * heads + h + 1) * 128]
            qb, kb = q.astype(BF), k.astype(BF)
            beta = col(beta_all, base + levels + 1)
            cc = col(clog, base + levels)
            end = clog_t[base + levels : base + levels + 1, n - 1 : n]
            crow = clog_t[base + levels : base + levels + 1, :]
            e = jnp.where(incl, jnp.exp(cc - crow), 0.0)
            s = (nt(qb, kb) * e).astype(BF)
            lp = jnp.where(strict, nt(kb, kb) * e, 0.0)
            lo = (lp * beta).astype(BF)
            e_ref[h] = e.astype(BF)
            s_ref[h] = s
            lp_ref[h] = lp.astype(BF)
            low[h % group] = lo
            tb[h] = jnp.where(row == lane, 1.0, 0.0).astype(BF) - lo * masks[0]
            grow = jnp.exp(cc)
            keep[h] = (grow * q, (v * beta).astype(BF), ((beta * grow) * k).astype(BF),
                       (jnp.exp(end - cc) * k).astype(BF), end)
        for level in range(1, masks.shape[0]):
            for h in hs:
                w = nn(low[h % group] * masks[level], tb[h]).astype(BF)
                tb[h] = tb[h] - nn(tb[h], w).astype(BF)
        for h in hs:
            base = h * LANES
            gq, vb, kbg, tk, end = keep[h]
            t_ref[h] = tb[h]
            m = nn(s_ref[h], tb[h])
            mb = m.astype(BF)
            m_ref[h] = mb
            mix = nn(tb[h], jnp.concatenate([vb, kbg], 1)).astype(BF)
            nk_ref[h] = mix
            au = tn(mix, tk)
            r2, l2 = iotas(128, 128)
            au_ref[h, 0:128] = au[0:128].astype(BF)
            au_ref[h, 128:256] = (jnp.where(r2 == l2, jnp.exp(end), 0.0) - au[128:256]).astype(BF)
            lam = jnp.where(cross < 64, col(lam_all, base),
                            jnp.where(cross < 128, col(lam_all, base + 1), col(lam_all, base + 2)))
            core_ref[h] = nn((m * lam).astype(BF), vb)
            qh_ref[h] = (gq - nn(mb, kbg)).astype(BF)


def local_forward(head_param, proj, gate, levels):
    rows = proj.shape[0]
    heads = head_param.shape[0]
    group = 2
    square = jax.ShapeDtypeStruct((heads, rows, rows), BF)
    bits = rows.bit_length() - 1
    return pl.pallas_call(
        functools.partial(local_kernel, heads, levels, group),
        in_specs=[pl.BlockSpec(memory_space=pltpu.SMEM), pl.BlockSpec(memory_space=VM), pl.BlockSpec(memory_space=VM)],
        out_specs=[pl.BlockSpec(memory_space=VM)] * 10,
        out_shape=[
            jax.ShapeDtypeStruct((heads, 256, 128), BF),
            square, square, square, square, square,
            jax.ShapeDtypeStruct((heads, rows, 256), BF),
            jax.ShapeDtypeStruct((heads, rows, 128), F32),
            jax.ShapeDtypeStruct((heads, rows, 128), BF),
            jax.ShapeDtypeStruct((rows, heads * LANES), F32),
        ],
        scratch_shapes=[VM((bits, rows, rows), BF), VM((group, rows, rows), BF)],
        name="local_forward",
    )(head_param, proj, gate)


def out_kernel(heads, levels, far, near, gate_ref, core_ref, qh_ref, x_ref, gain_ref, gout_ref, ow_ref,
               part_ref, g_ref, dqh_ref, gx_ref, dlam_ref):
    n = gate_ref.shape[0]
    lam_all = softplus(gate_ref[...])
    lane = lax.broadcasted_iota(jnp.int32, (n, heads * LANES), 1)
    gain = gain_ref[...]
    dlam = jnp.zeros((n, heads * LANES), F32)
    grad_normed = nt(gout_ref[...], ow_ref[...])
    normed = []
    for h in range(heads):
        base = h * LANES
        qh = qh_ref[h]
        x = x_ref[h]
        w = nt(qh, x)
        core = core_ref[h]
        fw = [col(lam_all, base + near + j) for j in range(far)]
        for j in range(far):
            core = core + fw[j] * w[:, j * 128 : (j + 1) * 128]
        rs = lax.rsqrt(jnp.mean(core * core, -1, keepdims=True) + 1e-06)
        unit_core = core * rs
        normed.append((unit_core * gain).astype(BF))
        gy = grad_normed[:, h * 128 : (h + 1) * 128] * gain
        g = rs * (gy - unit_core * jnp.mean(gy * unit_core, -1, keepdims=True))
        g_ref[h] = g.astype(BF)
        fg = jnp.concatenate([(fw[j] * g).astype(BF) for j in range(far)], 1)
        for j in range(far):
            here = jnp.sum(g * w[:, j * 128 : (j + 1) * 128], -1, keepdims=True)
            dlam = jnp.where(lane == base + near + j, here, dlam)
        dqh_ref[h] = nn(fg, x).astype(BF)
        gx_ref[h] = tn(fg, qh).astype(BF)
    dlam_ref[...] = dlam
    part_ref[...] = nn(jnp.concatenate(normed, 1), ow_ref[...]).astype(BF)


def out_stage(gate, core, qh, x, gain, grad_out, out_weight, levels, far, near):
    rows, width = grad_out.shape
    heads = core.shape[0]
    return pl.pallas_call(
        functools.partial(out_kernel, heads, levels, far, near),
        in_specs=[pl.BlockSpec(memory_space=VM)] * 7,
        out_specs=[pl.BlockSpec(memory_space=VM)] * 5,
        out_shape=[
            jax.ShapeDtypeStruct((rows, width), BF),
            jax.ShapeDtypeStruct((heads, rows, 128), BF),
            jax.ShapeDtypeStruct((heads, rows, 128), BF),
            jax.ShapeDtypeStruct((heads, far * 128, 128), BF),
            jax.ShapeDtypeStruct((rows, heads * LANES), F32),
        ],
        name="out_stage",
    )(gate, core, qh, x, gain, grad_out, out_weight)


def back_kernel(heads, levels, group, param_ref, proj_ref, gate_ref, clog_ref, e_ref, s_ref, lp_ref, t_ref, m_ref,
                nk_ref, g_ref, dqh_ref, dau_ref, dlam_ref, wflat_ref, swflat_ref, part_ref):
    n = proj_ref.shape[0]
    gate = gate_ref[...]
    rate, bias = head_rows(param_ref, heads, n)
    clog = clog_ref[...]
    beta_all = sigmoid(gate + bias)
    sig_all = sigmoid(gate)
    lam_all = softplus(gate)
    row, lane = iotas(n, n)
    cross = jnp.bitwise_xor(row, lane)
    strict = row > lane
    wide = lax.broadcasted_iota(jnp.int32, (n, heads * LANES), 1)
    dlam = dlam_ref[...]
    dlog = jnp.zeros((n, heads * LANES), F32)
    dbeta_all = jnp.zeros((n, heads * LANES), F32)
    last = lax.broadcasted_iota(jnp.int32, (n, 1), 0) == n - 1
    out = [None] * (3 * heads)
    for first in range(0, heads, group):
        for h in range(first, first + group):
            base = h * LANES
            q, rq = unit(proj_ref[:, h * 128 : (h + 1) * 128])
            k, rk = unit(proj_ref[:, (heads + h) * 128 : (heads + h + 1) * 128])
            v = proj_ref[:, (2 * heads + h) * 128 : (2 * heads + h + 1) * 128]
            qb, kb = q.astype(BF), k.astype(BF)
            beta = col(beta_all, base + levels + 1)
            cc = col(clog, base + levels)
            end = clog[n - 1 : n, base + levels : base + levels + 1]
            grow = jnp.exp(cc)
            tail = jnp.exp(end - cc)
            vb = (v * beta).astype(BF)
            kbg = ((beta * grow) * k).astype(BF)
            tk = (tail * k).astype(BF)
            g, dqh = g_ref[h], dqh_ref[h]
            mb, tb, mix = m_ref[h], t_ref[h], nk_ref[h]
            m = mb.astype(F32)
            lam = jnp.where(cross < 64, col(lam_all, base),
                            jnp.where(cross < 128, col(lam_all, base + 1), col(lam_all, base + 2)))
            dmw = nt(g, vb)
            prod = m * dmw
            zero = jnp.zeros_like(prod)
            for j, pick in enumerate((cross < 64, (cross >= 64) & (cross < 128), cross >= 128)):
                here = jnp.sum(jnp.where(pick, prod, zero), -1, keepdims=True)
                dlam = jnp.where(wide == base + j, here, dlam)
            mw = (m * lam).astype(BF)
            dm = (lam * dmw - nt(dqh, kbg)).astype(BF)
            dau = dau_ref[h]
            du, da = dau[0:128], dau[128:256]
            dnv = nt(tk, du)
            dkt = -nt(tk, da)
            dtk = nn(mix[:, 0:128], du) - nn(mix[:, 128:256], da)
            dmix = jnp.concatenate([dnv.astype(BF), dkt.astype(BF)], 1)
            back = tn(tb, dmix)
            dvb2, dkbg2 = back[:, 0:128], back[:, 128:256]
            dst = nt(dm, tb)
            dstb = dst.astype(BF)
            dvb = tn(mw, g) + dvb2
            both = tn(mb, jnp.concatenate([dqh, dstb], 1))
            dkbg = dkbg2 - both[:, 0:128]
            dlow = both[:, 128:] + nt(back.astype(BF), mix)
            dlow = jnp.where(strict, -dlow, 0.0)
            e = e_ref[h].astype(F32)
            dp = (dst * e).astype(BF)
            lp = lp_ref[h].astype(F32)
            dbeta = jnp.sum(dlow * lp, -1, keepdims=True)
            dkk = (dlow * (beta * e)).astype(BF)
            dq1 = nn(dp, kb)
            dk1 = tn(dp, qb)
            dk2 = nn(dkk, kb)
            dk3 = tn(dkk, kb)
            qr, kr = qb.astype(F32), kb.astype(F32)
            dqf, dtf, dkf = dqh.astype(F32), dtk, dkbg
            gq = jnp.sum(dqf * q, -1, keepdims=True)
            kk = jnp.sum(dkf * k, -1, keepdims=True)
            dtail = jnp.sum(dtf * k, -1, keepdims=True) * tail
            dc = jnp.sum(qr * dq1 + kr * (dk2 - dk1 - dk3), -1, keepdims=True)
            dc = dc + grow * (gq + beta * kk) - dtail
            r2, l2 = iotas(128, 128)
            trace = jnp.sum(jnp.where(r2 == l2, da.astype(F32), 0.0), keepdims=True)
            dend = jnp.sum(dtail, keepdims=True) + jnp.exp(end) * trace
            dc = dc + jnp.where(last, dend, 0.0)
            dbeta = dbeta + jnp.sum(dvb * v, -1, keepdims=True) + grow * kk
            dq = dq1 + grow * dqf
            dk = dk1 + dk2 + dk3 + (beta * grow) * dkf + tail * dtf
            dv = beta * dvb
            out[h] = (rq * (dq - q * jnp.sum(q * dq, -1, keepdims=True))).astype(BF)
            out[heads + h] = (rk * (dk - k * jnp.sum(k * dk, -1, keepdims=True))).astype(BF)
            out[2 * heads + h] = dv.astype(BF)
            dlog = jnp.where(wide == base + levels, dc, dlog)
            dbeta_all = jnp.where(wide == base + levels + 1, dbeta, dbeta_all)
    upper = jnp.where(lane >= row, 1.0, 0.0).astype(F32)
    dstep = lax.dot_general(upper, dlog, (((1,), (0,)), ((), ())),
                            precision=lax.Precision.HIGHEST, preferred_element_type=F32)
    dgate = dlam * sig_all - rate * sig_all * (1.0 - sig_all) * dstep + beta_all * (1.0 - beta_all) * dbeta_all
    dgate = dgate.astype(BF)
    dproj = jnp.concatenate(out, 1)
    width = part_ref.shape[1]
    for j in range(0, width, 512):
        part = nt(dproj, wflat_ref[j : j + 512, :]) + nt(dgate, swflat_ref[j : j + 512, :])
        part_ref[:, j : j + 512] = part.astype(BF)


def back_stage(head_param, proj, gate, clog, saved, g, dqh, dau, dlam, wflat, swflat, levels):
    rows = proj.shape[0]
    heads = head_param.shape[0]
    return pl.pallas_call(
        functools.partial(back_kernel, heads, levels, 1),
        in_specs=[pl.BlockSpec(memory_space=pltpu.SMEM)] + [pl.BlockSpec(memory_space=VM)] * 15,
        out_specs=pl.BlockSpec(memory_space=VM),
        out_shape=jax.ShapeDtypeStruct((rows, wflat.shape[0]), BF),
        compiler_params=pltpu.CompilerParams(vmem_limit_bytes=60 * 2**20),
        name="back_stage",
    )(head_param, proj, gate, clog, *saved, g, dqh, dau, dlam, wflat, swflat)


def swapped(array, axis, stride):
    return lax.ppermute(array, axis, [(i, i ^ 1 << stride) for i in range(lax.axis_size(axis))])


def mat_mul(left, right):
    return jnp.matmul(left, right)


def flip_last(array_in):
    return jnp.swapaxes(array_in, -1, -2)


def merge_step(pair_now, prefix, pair_peer, is_upper):
    a_now = pair_now[0]
    u_now = pair_now[1]
    a_peer = pair_peer[0]
    u_peer = pair_peer[1]
    arriving = jnp.where(is_upper, mat_mul(u_peer, prefix), 0.0)
    new_prefix = jnp.where(is_upper, mat_mul(a_peer, prefix), prefix)
    new_a = jnp.where(is_upper, mat_mul(a_peer, a_now), mat_mul(a_now, a_peer))
    new_u = jnp.where(is_upper, mat_mul(u_peer, a_now) + u_now, mat_mul(u_now, a_peer) + u_peer)
    return (arriving, new_prefix, jnp.stack([new_a, new_u], 0))


def on_device(tokens, qkv_weight, small_weight, head_param, norm_gain, out_weight, grad_out):
    rows, width = tokens.shape
    heads = qkv_weight.shape[2]
    levels = small_weight.shape[2] - 2
    near = (rows // 64).bit_length()
    far = lax.axis_size("ctx").bit_length() - 1
    index_ctx = lax.axis_index("ctx")
    proj, gate, wflat, swflat = project(tokens, qkv_weight, small_weight)
    au, *saved, core, qh, clog = local_forward(head_param, proj, gate, levels)
    au = au.astype(F32)
    pair_now = jnp.stack([au[:, 128:], au[:, :128]], 0)
    prefix = jnp.broadcast_to(jnp.eye(128, dtype=jnp.float32), (heads, 128, 128))
    saved_steps = []
    incoming = []
    for bit_no in range(far):
        pair_peer = swapped(pair_now.astype(BF), "ctx", bit_no).astype(F32)
        is_upper = index_ctx // 2**bit_no % 2 == 1
        saved_steps.append((pair_now, prefix, is_upper))
        arriving, prefix, pair_now = merge_step(pair_now, prefix, pair_peer, is_upper)
        incoming.append(arriving)
    x = jnp.concatenate(incoming, 1).astype(BF)
    out_part, g, dqh, gx, dlam = out_stage(
        gate, core, qh, x, norm_gain.reshape(1, -1), grad_out, out_weight.reshape(heads * 128, width),
        levels, far, near)
    layer_out = lax.psum_scatter(out_part, "head", scatter_dimension=1, tiled=True)
    gx = gx.astype(F32)
    grad_incoming = [gx[:, i * 128 : (i + 1) * 128] for i in range(far)]
    grad_pair = jnp.zeros_like(pair_now)
    grad_prefix = jnp.zeros(prefix.shape, F32)
    for bit_no in reversed(range(far)):
        pair_now, prefix, is_upper = saved_steps[bit_no]
        grad_arrived = grad_incoming[bit_no]
        through = jnp.stack(
            [mat_mul(grad_prefix, flip_last(prefix)), mat_mul(grad_arrived, flip_last(prefix))], 0)
        through = jnp.where(is_upper, through, 0.0)
        pair_peer, peer_grad, peer_through = (
            swapped(pair_now.astype(BF), "ctx", bit_no).astype(F32),
            swapped(grad_pair.astype(BF), "ctx", bit_no).astype(F32),
            swapped(through.astype(BF), "ctx", bit_no).astype(F32),
        )

        def step_local(pair_in, prefix_in, peer_in):
            return merge_step(pair_in, prefix_in, peer_in, is_upper)

        step_out, pull_step = jax.vjp(step_local, pair_now, prefix, pair_peer)
        own_part, grad_prefix, unused_peer = pull_step((grad_arrived, grad_prefix, grad_pair + peer_grad))
        grad_pair = own_part + peer_through
    dau = jnp.concatenate([grad_pair[1], grad_pair[0]], 1).astype(BF)
    grad_part = back_stage(head_param, proj, gate, clog, saved, g, dqh, dau, dlam, wflat, swflat, levels)
    grad_tokens = lax.psum_scatter(grad_part, "head", scatter_dimension=1, tiled=True)
    return (layer_out, grad_tokens)


def solution(mesh):
    placed = (
        P("ctx", None),
        P(None, None, "head", None),
        P(None, "head", None),
        P("head", None),
        P(),
        P("head", None, None),
        P("ctx", None),
    )
    return jax.shard_map(
        on_device,
        mesh=mesh,
        in_specs=placed,
        out_specs=(P("ctx", "head"), P("ctx", "head")),
        check_vma=False,
    )
```

```python
import functools

import jax
import jax.numpy as jnp
from jax import lax
from jax.experimental import pallas as pl
from jax.experimental.pallas import tpu as pltpu
from jax.sharding import PartitionSpec as P

BF = jnp.bfloat16
F32 = jnp.float32
LANES = 32
VM = pltpu.VMEM


def nn(a, b):
    return lax.dot_general(a, b, (((1,), (0,)), ((), ())), preferred_element_type=F32)


def nt(a, b):
    return lax.dot_general(a, b, (((1,), (1,)), ((), ())), preferred_element_type=F32)


def tn(a, b):
    return lax.dot_general(a, b, (((0,), (0,)), ((), ())), preferred_element_type=F32)


def sigmoid(x):
    return 1.0 / (1.0 + jnp.exp(-x))


def softplus(x):
    return jnp.maximum(x, 0.0) + jnp.log(1.0 + jnp.exp(-jnp.abs(x)))


def iotas(n, m):
    return lax.broadcasted_iota(jnp.int32, (n, m), 0), lax.broadcasted_iota(jnp.int32, (n, m), 1)


def col(array, lane):
    return array[:, lane : lane + 1]


def head_rows(param_ref, heads, rows):
    lane = lax.broadcasted_iota(jnp.int32, (rows, heads * LANES), 1)
    rate = jnp.zeros((rows, heads * LANES), F32)
    bias = jnp.zeros((rows, heads * LANES), F32)
    for h in range(heads):
        here = lane // LANES == h
        rate = jnp.where(here, param_ref[h, 0], rate)
        bias = jnp.where(here, param_ref[h, 1], bias)
    return rate, bias


def proj_kernel(heads, extra, tok_ref, w_ref, sw_ref, proj_ref, gate_ref, wflat_ref, swflat_ref, wide, swide):
    step = pl.program_id(0)
    parts = 3 * heads
    depth = tok_ref.shape[1]
    wide[...] = w_ref[...].astype(F32)
    swide[...] = sw_ref[...].astype(F32)
    for part in range(parts):
        wflat_ref[:, part * 128 : (part + 1) * 128] = wide[pl.ds(part, depth, stride=parts), :].astype(BF)
    swflat_ref[...] = jnp.zeros_like(swflat_ref)
    for h in range(heads):
        swflat_ref[:, h * LANES : h * LANES + extra] = swide[pl.ds(h, depth, stride=heads), :].astype(BF)

    @pl.when(step == 0)
    def _():
        proj_ref[...] = jnp.zeros_like(proj_ref)
        gate_ref[...] = jnp.zeros_like(gate_ref)

    tok = tok_ref[...]
    proj_ref[...] += nn(tok, wflat_ref[...])
    gate_ref[...] += nn(tok, swflat_ref[...])


def project(tokens, qkv_weight, small_weight):
    rows, width = tokens.shape
    heads = qkv_weight.shape[2]
    extra = small_weight.shape[2]
    parts = 3 * heads
    depth = 256
    return pl.pallas_call(
        functools.partial(proj_kernel, heads, extra),
        grid=(width // depth,),
        in_specs=[
            pl.BlockSpec((rows, depth), lambda i: (0, i)),
            pl.BlockSpec((depth * parts, 128), lambda i: (i, 0)),
            pl.BlockSpec((depth * heads, extra), lambda i: (i, 0)),
        ],
        out_specs=[
            pl.BlockSpec((rows, parts * 128), lambda i: (0, 0)),
            pl.BlockSpec((rows, heads * LANES), lambda i: (0, 0)),
            pl.BlockSpec((depth, parts * 128), lambda i: (i, 0)),
            pl.BlockSpec((depth, heads * LANES), lambda i: (i, 0)),
        ],
        out_shape=[
            jax.ShapeDtypeStruct((rows, parts * 128), F32),
            jax.ShapeDtypeStruct((rows, heads * LANES), F32),
            jax.ShapeDtypeStruct((width, parts * 128), BF),
            jax.ShapeDtypeStruct((width, heads * LANES), BF),
        ],
        scratch_shapes=[VM((depth * parts, 128), F32), VM((depth * heads, extra), F32)],
        name="project",
    )(tokens, qkv_weight.reshape(width * parts, 128), small_weight.reshape(width * heads, extra))


def unit(values):
    scale = lax.rsqrt(jnp.sum(values * values, -1, keepdims=True) + 1e-06)
    return values * scale, scale


def running_log(gate, rate, n):
    row, lane = iotas(n, n)
    lower = jnp.where(row >= lane, 1.0, 0.0).astype(F32)
    return lax.dot_general(
        lower, -rate * sigmoid(gate), (((1,), (0,)), ((), ())),
        precision=lax.Precision.HIGHEST, preferred_element_type=F32,
    )


def mask_rows(n, masks):
    row, lane = iotas(n, n)
    cross = jnp.bitwise_xor(row, lane)
    for k in range(masks.shape[0]):
        masks[k] = jnp.where(jnp.right_shift(cross, k) == 1, 1.0, 0.0).astype(BF)


def local_kernel(heads, levels, group, param_ref, proj_ref, gate_ref, au_ref, e_ref, s_ref, lp_ref, t_ref, m_ref,
                 nk_ref, core_ref, qh_ref, clog_ref, masks, low):
    n = proj_ref.shape[0]
    gate = gate_ref[...]
    rate, bias = head_rows(param_ref, heads, n)
    clog = running_log(gate, rate, n)
    clog_ref[...] = clog
    clog_t = clog.T
    beta_all = sigmoid(gate + bias)
    lam_all = softplus(gate)
    mask_rows(n, masks)
    row, lane = iotas(n, n)
    cross = jnp.bitwise_xor(row, lane)
    incl = row >= lane
    strict = row > lane
    half = n // 2
    for first in range(0, heads, group):
        hs = range(first, first + group)
        keep = {}
        tb = {}
        for h in hs:
            base = h * LANES
            q, _ = unit(proj_ref[:, h * 128 : (h + 1) * 128])
            k, _ = unit(proj_ref[:, (heads + h) * 128 : (heads + h + 1) * 128])
            v = proj_ref[:, (2 * heads + h) * 128 : (2 * heads + h + 1) * 128]
            qb, kb = q.astype(BF), k.astype(BF)
            beta = col(beta_all, base + levels + 1)
            cc = col(clog, base + levels)
            end = clog_t[base + levels : base + levels + 1, n - 1 : n]
            crow = clog_t[base + levels : base + levels + 1, :]
            e = jnp.where(incl, jnp.exp(cc - crow), 0.0)
            s = (nt(qb, kb) * e).astype(BF)
            lp = jnp.where(strict, nt(kb, kb) * e, 0.0)
            lo = (lp * beta).astype(BF)
            e_ref[h] = e.astype(BF)
            s_ref[h] = s
            lp_ref[h] = lp.astype(BF)
            low[h % group] = lo
            tb[h] = jnp.where(row == lane, 1.0, 0.0).astype(BF) - lo * masks[0]
            grow = jnp.exp(cc)
            keep[h] = (grow * q, (v * beta).astype(BF), ((beta * grow) * k).astype(BF),
                       (jnp.exp(end - cc) * k).astype(BF), end)
        for level in range(1, masks.shape[0]):
            for h in hs:
                w = nn(low[h % group] * masks[level], tb[h]).astype(BF)
                tb[h] = tb[h] - nn(tb[h], w).astype(BF)
        for h in hs:
            base = h * LANES
            gq, vb, kbg, tk, end = keep[h]
            t_ref[h] = tb[h]
            m = nn(s_ref[h], tb[h])
            mb = m.astype(BF)
            m_ref[h] = mb
            mix = nn(tb[h], jnp.concatenate([vb, kbg], 1)).astype(BF)
            nk_ref[h] = mix
            au = tn(mix, tk)
            r2, l2 = iotas(128, 128)
            au_ref[h, 0:128] = au[0:128].astype(BF)
            au_ref[h, 128:256] = (jnp.where(r2 == l2, jnp.exp(end), 0.0) - au[128:256]).astype(BF)
            lam = jnp.where(cross < 64, col(lam_all, base),
                            jnp.where(cross < 128, col(lam_all, base + 1), col(lam_all, base + 2)))
            core_ref[h] = nn((m * lam).astype(BF), vb)
            qh_ref[h] = (gq - nn(mb, kbg)).astype(BF)


def local_forward(head_param, proj, gate, levels):
    rows = proj.shape[0]
    heads = head_param.shape[0]
    group = 2
    square = jax.ShapeDtypeStruct((heads, rows, rows), BF)
    bits = rows.bit_length() - 1
    return pl.pallas_call(
        functools.partial(local_kernel, heads, levels, group),
        in_specs=[pl.BlockSpec(memory_space=pltpu.SMEM), pl.BlockSpec(memory_space=VM), pl.BlockSpec(memory_space=VM)],
        out_specs=[pl.BlockSpec(memory_space=VM)] * 10,
        out_shape=[
            jax.ShapeDtypeStruct((heads, 256, 128), BF),
            square, square, square, square, square,
            jax.ShapeDtypeStruct((heads, rows, 256), BF),
            jax.ShapeDtypeStruct((heads, rows, 128), F32),
            jax.ShapeDtypeStruct((heads, rows, 128), BF),
            jax.ShapeDtypeStruct((rows, heads * LANES), F32),
        ],
        scratch_shapes=[VM((bits, rows, rows), BF), VM((group, rows, rows), BF)],
        name="local_forward",
    )(head_param, proj, gate)


def out_kernel(heads, levels, far, near, gate_ref, core_ref, qh_ref, x_ref, gain_ref, gout_ref, ow_ref,
               part_ref, g_ref, dqh_ref, gx_ref, dlam_ref):
    n = gate_ref.shape[0]
    lam_all = softplus(gate_ref[...])
    lane = lax.broadcasted_iota(jnp.int32, (n, heads * LANES), 1)
    gain = gain_ref[...]
    dlam = jnp.zeros((n, heads * LANES), F32)
    grad_normed = nt(gout_ref[...], ow_ref[...])
    normed = []
    for h in range(heads):
        base = h * LANES
        qh = qh_ref[h]
        x = x_ref[h]
        w = nt(qh, x)
        core = core_ref[h]
        fw = [col(lam_all, base + near + j) for j in range(far)]
        for j in range(far):
            core = core + fw[j] * w[:, j * 128 : (j + 1) * 128]
        rs = lax.rsqrt(jnp.mean(core * core, -1, keepdims=True) + 1e-06)
        unit_core = core * rs
        normed.append((unit_core * gain).astype(BF))
        gy = grad_normed[:, h * 128 : (h + 1) * 128] * gain
        g = rs * (gy - unit_core * jnp.mean(gy * unit_core, -1, keepdims=True))
        g_ref[h] = g.astype(BF)
        fg = jnp.concatenate([(fw[j] * g).astype(BF) for j in range(far)], 1)
        for j in range(far):
            here = jnp.sum(g * w[:, j * 128 : (j + 1) * 128], -1, keepdims=True)
            dlam = jnp.where(lane == base + near + j, here, dlam)
        dqh_ref[h] = nn(fg, x).astype(BF)
        gx_ref[h] = tn(fg, qh).astype(BF)
    dlam_ref[...] = dlam
    normed = jnp.concatenate(normed, 1)
    wide = part_ref.shape[2]
    for j in range(part_ref.shape[0]):
        part_ref[j] = nn(normed, ow_ref[:, j * wide : (j + 1) * wide]).astype(BF)


def out_stage(gate, core, qh, x, gain, grad_out, out_weight, levels, far, near, groups):
    rows, width = grad_out.shape
    heads = core.shape[0]
    return pl.pallas_call(
        functools.partial(out_kernel, heads, levels, far, near),
        in_specs=[pl.BlockSpec(memory_space=VM)] * 7,
        out_specs=[pl.BlockSpec(memory_space=VM)] * 5,
        out_shape=[
            jax.ShapeDtypeStruct((groups, rows, width // groups), BF),
            jax.ShapeDtypeStruct((heads, rows, 128), BF),
            jax.ShapeDtypeStruct((heads, rows, 128), BF),
            jax.ShapeDtypeStruct((heads, far * 128, 128), BF),
            jax.ShapeDtypeStruct((rows, heads * LANES), F32),
        ],
        name="out_stage",
    )(gate, core, qh, x, gain, grad_out, out_weight)


def back_kernel(heads, levels, group, param_ref, proj_ref, gate_ref, clog_ref, e_ref, s_ref, lp_ref, t_ref, m_ref,
                nk_ref, g_ref, dqh_ref, dau_ref, dlam_ref, dproj_ref, dgate_ref):
    n = proj_ref.shape[0]
    gate = gate_ref[...]
    rate, bias = head_rows(param_ref, heads, n)
    clog = clog_ref[...]
    beta_all = sigmoid(gate + bias)
    sig_all = sigmoid(gate)
    lam_all = softplus(gate)
    row, lane = iotas(n, n)
    cross = jnp.bitwise_xor(row, lane)
    strict = row > lane
    wide = lax.broadcasted_iota(jnp.int32, (n, heads * LANES), 1)
    dlam = dlam_ref[...]
    dlog = jnp.zeros((n, heads * LANES), F32)
    dbeta_all = jnp.zeros((n, heads * LANES), F32)
    last = lax.broadcasted_iota(jnp.int32, (n, 1), 0) == n - 1
    out = [None] * (3 * heads)
    for first in range(0, heads, group):
        for h in range(first, first + group):
            base = h * LANES
            q, rq = unit(proj_ref[:, h * 128 : (h + 1) * 128])
            k, rk = unit(proj_ref[:, (heads + h) * 128 : (heads + h + 1) * 128])
            v = proj_ref[:, (2 * heads + h) * 128 : (2 * heads + h + 1) * 128]
            qb, kb = q.astype(BF), k.astype(BF)
            beta = col(beta_all, base + levels + 1)
            cc = col(clog, base + levels)
            end = clog[n - 1 : n, base + levels : base + levels + 1]
            grow = jnp.exp(cc)
            tail = jnp.exp(end - cc)
            vb = (v * beta).astype(BF)
            kbg = ((beta * grow) * k).astype(BF)
            tk = (tail * k).astype(BF)
            g, dqh = g_ref[h], dqh_ref[h]
            mb, tb, mix = m_ref[h], t_ref[h], nk_ref[h]
            m = mb.astype(F32)
            lam = jnp.where(cross < 64, col(lam_all, base),
                            jnp.where(cross < 128, col(lam_all, base + 1), col(lam_all, base + 2)))
            dmw = nt(g, vb)
            prod = m * dmw
            zero = jnp.zeros_like(prod)
            for j, pick in enumerate((cross < 64, (cross >= 64) & (cross < 128), cross >= 128)):
                here = jnp.sum(jnp.where(pick, prod, zero), -1, keepdims=True)
                dlam = jnp.where(wide == base + j, here, dlam)
            mw = (m * lam).astype(BF)
            dm = (lam * dmw - nt(dqh, kbg)).astype(BF)
            dau = dau_ref[h]
            du, da = dau[0:128], dau[128:256]
            dnv = nt(tk, du)
            dkt = -nt(tk, da)
            dtk = nn(mix[:, 0:128], du) - nn(mix[:, 128:256], da)
            dmix = jnp.concatenate([dnv.astype(BF), dkt.astype(BF)], 1)
            back = tn(tb, dmix)
            dvb2, dkbg2 = back[:, 0:128], back[:, 128:256]
            dst = nt(dm, tb)
            dstb = dst.astype(BF)
            dvb = tn(mw, g) + dvb2
            both = tn(mb, jnp.concatenate([dqh, dstb], 1))
            dkbg = dkbg2 - both[:, 0:128]
            dlow = both[:, 128:] + nt(back.astype(BF), mix)
            dlow = jnp.where(strict, -dlow, 0.0)
            e = e_ref[h].astype(F32)
            dp = (dst * e).astype(BF)
            lp = lp_ref[h].astype(F32)
            dbeta = jnp.sum(dlow * lp, -1, keepdims=True)
            dkk = (dlow * (beta * e)).astype(BF)
            dq1 = nn(dp, kb)
            dk1 = tn(dp, qb)
            dk2 = nn(dkk, kb)
            dk3 = tn(dkk, kb)
            qr, kr = qb.astype(F32), kb.astype(F32)
            dqf, dtf, dkf = dqh.astype(F32), dtk, dkbg
            gq = jnp.sum(dqf * q, -1, keepdims=True)
            kk = jnp.sum(dkf * k, -1, keepdims=True)
            dtail = jnp.sum(dtf * k, -1, keepdims=True) * tail
            dc = jnp.sum(qr * dq1 + kr * (dk2 - dk1 - dk3), -1, keepdims=True)
            dc = dc + grow * (gq + beta * kk) - dtail
            r2, l2 = iotas(128, 128)
            trace = jnp.sum(jnp.where(r2 == l2, da.astype(F32), 0.0), keepdims=True)
            dend = jnp.sum(dtail, keepdims=True) + jnp.exp(end) * trace
            dc = dc + jnp.where(last, dend, 0.0)
            dbeta = dbeta + jnp.sum(dvb * v, -1, keepdims=True) + grow * kk
            dq = dq1 + grow * dqf
            dk = dk1 + dk2 + dk3 + (beta * grow) * dkf + tail * dtf
            dv = beta * dvb
            out[h] = (rq * (dq - q * jnp.sum(q * dq, -1, keepdims=True))).astype(BF)
            out[heads + h] = (rk * (dk - k * jnp.sum(k * dk, -1, keepdims=True))).astype(BF)
            out[2 * heads + h] = dv.astype(BF)
            dlog = jnp.where(wide == base + levels, dc, dlog)
            dbeta_all = jnp.where(wide == base + levels + 1, dbeta, dbeta_all)
    upper = jnp.where(lane >= row, 1.0, 0.0).astype(F32)
    dstep = lax.dot_general(upper, dlog, (((1,), (0,)), ((), ())),
                            precision=lax.Precision.HIGHEST, preferred_element_type=F32)
    dgate = dlam * sig_all - rate * sig_all * (1.0 - sig_all) * dstep + beta_all * (1.0 - beta_all) * dbeta_all
    dgate_ref[...] = dgate.astype(BF)
    for j, grad in enumerate(out):
        dproj_ref[:, j * 128 : (j + 1) * 128] = grad


def back_stage(head_param, proj, gate, clog, saved, g, dqh, dau, dlam, levels):
    rows = proj.shape[0]
    heads = head_param.shape[0]
    return pl.pallas_call(
        functools.partial(back_kernel, heads, levels, 1),
        in_specs=[pl.BlockSpec(memory_space=pltpu.SMEM)] + [pl.BlockSpec(memory_space=VM)] * 13,
        out_specs=[pl.BlockSpec(memory_space=VM)] * 2,
        out_shape=[jax.ShapeDtypeStruct((rows, 3 * heads * 128), BF), jax.ShapeDtypeStruct((rows, heads * LANES), BF)],
        name="back_stage",
    )(head_param, proj, gate, clog, *saved, g, dqh, dau, dlam)


MESH = pl.DeviceIdType.MESH
RING = 4


def place():
    ctx = lax.axis_index("ctx")
    return lax.div(ctx, 2 * RING), lax.rem(lax.div(ctx, 2), RING), lax.rem(ctx, 2)


def at_ctx(x, y, core):
    return {"ctx": (x * RING + y) * 2 + core}


def around(index, step):
    return lax.rem(index + step + RING, RING)


def greet(peers):
    barrier = pltpu.get_barrier_semaphore()
    for peer in peers:
        pl.semaphore_signal(barrier, inc=1, device_id=peer, device_id_type=MESH)
    pl.semaphore_wait(barrier, len(peers))


def remote(src, dst, send, recv, index, peer):
    return pltpu.make_async_remote_copy(
        src_ref=src, dst_ref=dst, send_sem=send.at[index], recv_sem=recv.at[index],
        device_id=peer, device_id_type=MESH)


def ring_start(buf, send, recv, base, right, left, low=0):
    rows = pl.ds(low, buf.shape[2] - low)
    copies = [
        remote(buf.at[0, 0, rows], buf.at[1, 0, rows], send, recv, base, right),
        remote(buf.at[0, 1], buf.at[3, 1], send, recv, base + 1, left),
        remote(buf.at[0, 1, rows], buf.at[1, 1, rows], send, recv, base + 2, right),
        remote(buf.at[0, 0], buf.at[3, 0], send, recv, base + 3, left),
    ]
    for copy in copies:
        copy.start()
    return copies


def ring_finish(copies, buf, send, recv, base, right, left, low=0):
    rows = pl.ds(low, buf.shape[2] - low)
    copies[0].wait_recv()
    on_right = remote(buf.at[1, 0, rows], buf.at[2, 0, rows], send, recv, base + 4, right)
    on_right.start()
    copies[1].wait_recv()
    on_left = remote(buf.at[3, 1, rows], buf.at[2, 1, rows], send, recv, base + 5, left)
    on_left.start()
    copies[2].wait_recv()
    copies[3].wait_recv()
    on_right.wait_recv()
    on_left.wait_recv()
    for copy in copies + [on_right, on_left]:
        copy.wait_send()


def flag(cond):
    return jnp.where(cond, 1.0, 0.0).astype(F32)


def gather_kernel(au_ref, x_ref, cores_ref, ys_ref, xs_ref, cores, ys, xs, share, send, recv, local):
    x, y, core = place()
    partner = at_ctx(x, y, 1 - core)
    y_right, y_left = at_ctx(x, around(y, 1), core), at_ctx(x, around(y, -1), core)
    x_right, x_left = at_ctx(around(x, 1), y, core), at_ctx(around(x, -1), y, core)
    greet((partner, y_right, y_left, x_right, x_left))
    swap = remote(au_ref, cores.at[1], send, recv, 0, partner)
    swap.start()
    keep = pltpu.make_async_copy(au_ref, cores.at[0], local.at[0])
    keep.start()
    keep.wait()
    swap.wait_recv()
    first = core * 2
    low_slot, high_slot = core, 1 - core
    eye_r, eye_c = iotas(128, 128)
    eye = jnp.where(eye_r == eye_c, 1.0, 0.0).astype(F32)
    top = lax.broadcasted_iota(jnp.int32, (256, 128), 0) < 128

    def joined(below, above):
        return nn(below, above[128:256]) + jnp.where(top, above.astype(F32), 0.0)

    for i in range(2):
        ys[0, i] = joined(cores[low_slot, first + i], cores[high_slot, first + i]).astype(BF)
    copies = ring_start(ys, send, recv, 1, y_right, y_left)
    ring_finish(copies, ys, send, recv, 1, y_right, y_left)
    prefix = [None, None]
    for i in range(2):
        at = [ys[around(y, -k), i] for k in range(RING)]
        s1 = joined(at[0], at[1])
        s2 = joined(s1.astype(BF), at[2])
        s3 = joined(s2.astype(BF), at[3])
        xs[0, i] = s3.astype(BF)
        x1 = flag(lax.rem(y, 2) == 1) * ys[1, i, 0:128].astype(F32)
        s1u = s1[0:128]
        x2 = flag(y == 2) * s1u + flag(y == 3) * nn(s1u.astype(BF), at[2][128:256])
        share[first + i, 0:128] = x1.astype(BF)
        share[first + i, 128:256] = x2.astype(BF)
        prefix[i] = (flag(y == 0) * eye + flag(y == 1) * at[0][128:256].astype(F32)
                     + flag(y == 2) * s1[128:256] + flag(y == 3) * s2[128:256]).astype(BF)
    copies = ring_start(xs, send, recv, 7, x_right, x_left)
    ring_finish(copies, xs, send, recv, 7, x_right, x_left)
    for i in range(2):
        at = [xs[around(x, -k), i] for k in range(RING)]
        r1 = nn(at[0][0:128], at[1][128:256]) + at[1][0:128].astype(F32)
        x3 = flag(lax.rem(x, 2) == 1) * xs[1, i, 0:128].astype(F32)
        x4 = flag(x == 2) * r1 + flag(x == 3) * nn(r1.astype(BF), at[2][128:256])
        both = jnp.concatenate([x3.astype(BF), x4.astype(BF)], 0)
        share[first + i, 256:512] = nn(both, prefix[i]).astype(BF)
    give = remote(share.at[pl.ds(first, 2)], share.at[pl.ds(first, 2)], send, recv, 13, partner)
    take = remote(share.at[pl.ds(2 - first, 2)], share.at[pl.ds(2 - first, 2)], send, recv, 13, partner)
    give.start()
    upper = flag(core == 1)
    swap.wait_send()
    step = []
    for h in range(4):
        below = cores[low_slot, h]
        x_ref[h, 0:128] = (upper * below[0:128].astype(F32)).astype(BF)
        step.append((upper * below[128:256].astype(F32) + (1.0 - upper) * eye).astype(BF))
    cores_ref[...] = cores[...]
    ys_ref[...] = ys[...]
    xs_ref[...] = xs[...]
    take.wait_recv()
    give.wait_send()
    for h in range(4):
        x_ref[h, 128:640] = nn(share[h], step[h]).astype(BF)


def gather_states(au):
    heads = au.shape[0]
    cores = ((2, heads, 256, 128), BF)
    ring = ((RING, 2, 256, 128), BF)
    return pl.pallas_call(
        gather_kernel,
        in_specs=[pl.BlockSpec(memory_space=VM)],
        out_specs=[pl.BlockSpec(memory_space=VM)] * 4,
        out_shape=[jax.ShapeDtypeStruct((heads, 640, 128), BF)] + [jax.ShapeDtypeStruct(*s) for s in (cores, ring, ring)],
        scratch_shapes=[VM(*cores), VM(*ring), VM(*ring), VM((heads, 512, 128), BF),
                        pltpu.SemaphoreType.DMA((14,)), pltpu.SemaphoreType.DMA((14,)), pltpu.SemaphoreType.DMA((1,))],
        compiler_params=pltpu.CompilerParams(collective_id=1, has_side_effects=True),
        name="gather_states",
    )(au)


def return_kernel(groups, gx_ref, x_ref, cores_ref, ys_ref, xs_ref, part_ref, dau_ref, layer_ref,
                  mine, other, ys, xs, share, chunks, send, recv, zsend, zrecv):
    x, y, core = place()
    z = lax.axis_index("head")
    partner = at_ctx(x, y, 1 - core)
    y_right, y_left = at_ctx(x, around(y, 1), core), at_ctx(x, around(y, -1), core)
    x_right, x_left = at_ctx(around(x, 1), y, core), at_ctx(around(x, -1), y, core)
    across = [{"head": lax.rem(z + k, groups)} for k in range(1, groups)]
    greet([partner, y_right, y_left, x_right, x_left] + across)
    first = core * 2
    rest = 2 - first
    swap = remote(gx_ref.at[pl.ds(rest, 2)], mine, send, recv, 0, partner)
    swap.start()
    swap_rest = remote(gx_ref.at[pl.ds(first, 2)], other, send, recv, 1, partner)
    swap_rest.start()
    spread = []
    for k in range(1, groups):
        to = lax.rem(z + k, groups)
        spread.append(remote(part_ref.at[to], chunks.at[k - 1], zsend, zrecv, k - 1, across[k - 1]))
        spread[-1].start()
    low_slot, high_slot = core, 1 - core
    upper = flag(core == 1)
    bits = [flag(core == 1), flag(lax.rem(y, 2) == 1), flag(y >= 2), flag(lax.rem(x, 2) == 1), flag(x >= 2)]
    eye_r, eye_c = iotas(128, 128)
    eye = jnp.where(eye_r == eye_c, 1.0, 0.0).astype(F32)
    level = lax.div(lax.broadcasted_iota(jnp.int32, (512, 128), 0), 128)
    mask = jnp.where(level == 0, bits[1], jnp.where(level == 1, bits[2], jnp.where(level == 2, bits[3], bits[4])))
    swap.wait_recv()
    for i in range(2):
        here = gx_ref[first + i, 128:640]
        there = mine[i, 128:640]
        high = (upper * here.astype(F32) + (1.0 - upper) * there.astype(F32)).astype(BF)
        low = (1.0 - upper) * here.astype(F32) + upper * there.astype(F32)
        ys[0, i] = (mask * (low + nt(high, cores_ref[low_slot, first + i, 128:256]))).astype(BF)
    copies = ring_start(ys, send, recv, 2, y_right, y_left, 128)
    after = [None, None]
    for i in range(2):
        at = [ys_ref[around(y, -k), i, 128:256] for k in range(RING)]
        q1 = nn(at[2], at[3])
        q0 = nn(at[1], q1.astype(BF))
        after[i] = (flag(y == 3) * eye + flag(y == 2) * at[3].astype(F32) + flag(y == 1) * q1 + flag(y == 0) * q0).astype(BF)
    ring_finish(copies, ys, send, recv, 2, y_right, y_left, 128)
    held = [None, None]
    for i in range(2):
        trans = [ys_ref[around(y, -k), i, 128:256] for k in range(RING)]
        at = [ys[around(y, -k), i, 128:512] for k in range(RING)]
        h1 = nt(at[3], trans[2]) + at[2].astype(F32)
        h0 = nt(h1.astype(BF), trans[1]) + at[1].astype(F32)
        column = nt(h0[128:384].astype(BF), trans[0]) + at[0][128:384].astype(F32)
        xs[0, i] = column.astype(BF)
        held[i] = flag(y == 2) * at[3].astype(F32) + flag(y == 1) * h1 + flag(y == 0) * h0
        share[first + i, 0:128] = ((1.0 - bits[1]) * ys[3, i, 0:128].astype(F32)).astype(BF)
        share[first + i, 128:256] = held[i][0:128].astype(BF)
    copies = ring_start(xs, send, recv, 8, x_right, x_left)
    ring_finish(copies, xs, send, recv, 8, x_right, x_left)
    for i in range(2):
        trans = [xs_ref[around(x, -k), i, 128:256] for k in range(RING)]
        at = [xs[around(x, -k), i, 128:256] for k in range(RING)]
        h1 = nt(at[3], trans[2]) + at[2].astype(F32)
        h0 = nt(h1.astype(BF), trans[1]) + at[1].astype(F32)
        v4 = flag(x == 2) * at[3].astype(F32) + flag(x == 1) * h1 + flag(x == 0) * h0
        v3 = (1.0 - bits[3]) * xs[3, i, 0:128].astype(F32)
        both = jnp.concatenate([v3.astype(BF), v4.astype(BF)], 0)
        share[first + i, 256:512] = (held[i][128:384] + nt(both, after[i])).astype(BF)
    give = remote(share.at[pl.ds(first, 2)], share.at[pl.ds(first, 2)], send, recv, 14, partner)
    take = remote(share.at[pl.ds(rest, 2)], share.at[pl.ds(rest, 2)], send, recv, 14, partner)
    give.start()
    swap_rest.wait_recv()
    take.wait_recv()
    give.wait_send()
    for h in range(4):
        mine_here = flag(core == h // 2)
        got = mine_here * mine[h % 2].astype(F32) + (1.0 - mine_here) * other[h % 2].astype(F32)
        got = (1.0 - upper) * got
        v0 = got[0:128]
        move = (upper * eye + (1.0 - upper) * cores_ref[high_slot, h, 128:256].astype(F32)).astype(BF)
        v = nt(share[h], move) + mask * got[128:640]
        parts = [v0] + [v[k * 128 : (k + 1) * 128] for k in range(4)]
        so_far = jnp.zeros((128, 128), F32)
        du = jnp.zeros((128, 128), F32)
        states = []
        for k in range(5):
            state = x_ref[h, k * 128 : (k + 1) * 128].astype(F32)
            states.append((bits[k] * state + (1.0 - bits[k]) * so_far).astype(BF))
            so_far = so_far + state
            du = du + (1.0 - bits[k]) * parts[k]
        da = tn(jnp.concatenate(states, 0), jnp.concatenate([v0, v], 0).astype(BF))
        dau_ref[h, 0:128] = du.astype(BF)
        dau_ref[h, 128:256] = da.astype(BF)
    total = part_ref[z].astype(F32)
    for copy in spread:
        copy.wait_recv()
    for k in range(groups - 1):
        total = total + chunks[k].astype(F32)
    layer_ref[...] = total.astype(BF)
    for copy in [swap, swap_rest] + spread:
        copy.wait_send()


def return_grads(gx, x, cores, ys, xs, part):
    heads = gx.shape[0]
    groups, rows, wide = part.shape
    ring = (RING, 2)
    return pl.pallas_call(
        functools.partial(return_kernel, groups),
        in_specs=[pl.BlockSpec(memory_space=VM)] * 6,
        out_specs=[pl.BlockSpec(memory_space=VM)] * 2,
        out_shape=[jax.ShapeDtypeStruct((heads, 256, 128), BF), jax.ShapeDtypeStruct((rows, wide), BF)],
        scratch_shapes=[VM((2, 640, 128), BF), VM((2, 640, 128), BF), VM(ring + (512, 128), BF), VM(ring + (256, 128), BF),
                        VM((heads, 512, 128), BF), VM((3, rows, wide), BF),
                        pltpu.SemaphoreType.DMA((15,)), pltpu.SemaphoreType.DMA((15,)),
                        pltpu.SemaphoreType.DMA((3,)), pltpu.SemaphoreType.DMA((3,))],
        compiler_params=pltpu.CompilerParams(collective_id=2, has_side_effects=True),
        name="return_grads",
    )(gx, x, cores, ys, xs, part)


def last_kernel(groups, dproj_ref, dgate_ref, w_ref, sw_ref, out_ref, mine, relay, direct, extra, arrive, send, recv):
    rows, wide = out_ref.shape
    z = lax.axis_index("head")
    half = wide // 2
    right, left = {"head": lax.rem(z + 1, groups)}, {"head": lax.rem(z + groups - 1, groups)}
    greet((right, left))
    dproj, dgate = dproj_ref[...], dgate_ref[...]

    def product(step):
        chunk = lax.rem(z + step + groups, groups)
        at = pl.ds(pl.multiple_of(chunk * wide, wide), wide)
        return nt(dproj, w_ref[at, :]) + nt(dgate, sw_ref[at, :])

    far = product(2)
    relay[0] = far[:, :half].astype(BF)
    relay[1] = far[:, half:].astype(BF)
    far_right = remote(relay.at[0], arrive.at[0], send, recv, 0, right)
    far_left = remote(relay.at[1], arrive.at[1], send, recv, 1, left)
    far_right.start()
    far_left.start()
    to_right = product(1)
    direct[0] = to_right[:, half:].astype(BF)
    near_right = remote(direct.at[0], arrive.at[2], send, recv, 2, right)
    near_right.start()
    to_left = product(-1)
    direct[1] = to_left[:, :half].astype(BF)
    near_left = remote(direct.at[1], arrive.at[3], send, recv, 3, left)
    near_left.start()
    far_right.wait_recv()
    extra[0] = (to_right[:, :half] + arrive[0].astype(F32)).astype(BF)
    sum_right = remote(extra.at[0], arrive.at[4], send, recv, 4, right)
    sum_right.start()
    far_left.wait_recv()
    extra[1] = (to_left[:, half:] + arrive[1].astype(F32)).astype(BF)
    sum_left = remote(extra.at[1], arrive.at[5], send, recv, 5, left)
    sum_left.start()
    mine[...] = product(0)
    near_right.wait_recv()
    near_left.wait_recv()
    sum_right.wait_recv()
    sum_left.wait_recv()
    out_ref[:, :half] = (mine[:, :half] + arrive[4].astype(F32) + arrive[3].astype(F32)).astype(BF)
    out_ref[:, half:] = (mine[:, half:] + arrive[5].astype(F32) + arrive[2].astype(F32)).astype(BF)
    for copy in (far_right, far_left, near_right, near_left, sum_right, sum_left):
        copy.wait_send()


def last_stage(dproj, dgate, wflat, swflat, groups):
    rows = dproj.shape[0]
    wide = wflat.shape[0] // groups
    half = (rows, wide // 2)
    return pl.pallas_call(
        functools.partial(last_kernel, groups),
        in_specs=[pl.BlockSpec(memory_space=VM)] * 4,
        out_specs=pl.BlockSpec(memory_space=VM),
        out_shape=jax.ShapeDtypeStruct((rows, wide), BF),
        scratch_shapes=[VM((rows, wide), F32), VM((2,) + half, BF), VM((2,) + half, BF), VM((2,) + half, BF),
                        VM((6,) + half, BF), pltpu.SemaphoreType.DMA((6,)), pltpu.SemaphoreType.DMA((6,))],
        compiler_params=pltpu.CompilerParams(collective_id=3, has_side_effects=True),
        name="last_stage",
    )(dproj, dgate, wflat, swflat)


def on_device(tokens, qkv_weight, small_weight, head_param, norm_gain, out_weight, grad_out):
    rows, width = tokens.shape
    heads = qkv_weight.shape[2]
    levels = small_weight.shape[2] - 2
    near = (rows // 64).bit_length()
    far = lax.axis_size("ctx").bit_length() - 1
    groups = lax.axis_size("head")
    proj, gate, wflat, swflat = project(tokens, qkv_weight, small_weight)
    au, *saved, core, qh, clog = local_forward(head_param, proj, gate, levels)
    x, cores, ys, xs = gather_states(au)
    part, g, dqh, gx, dlam = out_stage(
        gate, core, qh, x, norm_gain.reshape(1, -1), grad_out, out_weight.reshape(heads * 128, width),
        levels, far, near, groups)
    dau, layer_out = return_grads(gx, x, cores, ys, xs, part)
    dproj, dgate = back_stage(head_param, proj, gate, clog, saved, g, dqh, dau, dlam, levels)
    grad_tokens = last_stage(dproj, dgate, wflat, swflat, groups)
    return (layer_out, grad_tokens)


def solution(mesh):
    placed = (
        P("ctx", None),
        P(None, None, "head", None),
        P(None, "head", None),
        P("head", None),
        P(),
        P("head", None, None),
        P("ctx", None),
    )
    return jax.shard_map(
        on_device,
        mesh=mesh,
        in_specs=placed,
        out_specs=(P("ctx", "head"), P("ctx", "head")),
        check_vma=False,
    )
```

```python
import functools

import jax
import jax.numpy as jnp
from jax import lax
from jax.experimental import pallas as pl
from jax.experimental.pallas import tpu as pltpu
from jax.sharding import PartitionSpec as P

BF = jnp.bfloat16
F32 = jnp.float32
LANES = 32
LIMIT = {"project": 44, "local": 24, "gather": 16, "out": 16, "return": 20, "back": 24, "last": 24}


def lane_of(h, level, heads):
    return level * heads + h
VM = pltpu.VMEM


def nn(a, b):
    return lax.dot_general(a, b, (((1,), (0,)), ((), ())), preferred_element_type=F32)


def nt(a, b):
    return lax.dot_general(a, b, (((1,), (1,)), ((), ())), preferred_element_type=F32)


def tn(a, b):
    return lax.dot_general(a, b, (((0,), (0,)), ((), ())), preferred_element_type=F32)


def sigmoid(x):
    return 1.0 / (1.0 + jnp.exp(-x))


def softplus(x):
    return jnp.maximum(x, 0.0) + jnp.log(1.0 + jnp.exp(-jnp.abs(x)))


def iotas(n, m):
    return lax.broadcasted_iota(jnp.int32, (n, m), 0), lax.broadcasted_iota(jnp.int32, (n, m), 1)


def col(array, lane):
    return array[:, lane : lane + 1]


def head_rows(param_ref, heads, rows):
    lane = lax.broadcasted_iota(jnp.int32, (rows, heads * LANES), 1)
    rate = jnp.zeros((rows, heads * LANES), F32)
    bias = jnp.zeros((rows, heads * LANES), F32)
    for h in range(heads):
        here = lane % heads == h
        rate = jnp.where(here, param_ref[0, h], rate)
        bias = jnp.where(here, param_ref[1, h], bias)
    return rate, bias


def proj_kernel(heads, depth, tok_hbm, w_hbm, sw_hbm, proj_ref, gate_ref, wflat_ref, swt_ref, tok_ref, w_ref, sw_ref, wide, swide, sems):
    parts = 3 * heads
    steps = w_ref.shape[0]
    span = depth * parts
    tok_copy = pltpu.make_async_copy(tok_hbm, tok_ref, sems.at[steps])
    sw_copy = pltpu.make_async_copy(sw_hbm, sw_ref, sems.at[steps + 1])
    copies = [pltpu.make_async_copy(w_hbm.at[pl.ds(i * span, span)], w_ref.at[i], sems.at[i]) for i in range(steps)]
    copies[0].start()
    tok_copy.start()
    for copy in copies[1:]:
        copy.start()
    sw_copy.start()
    for i in range(steps):
        copies[i].wait()
        rows = pl.ds(i * depth, depth)
        wide[i % 2] = w_ref[i].astype(F32)
        for part in range(parts):
            wflat_ref[rows, part * 128 : (part + 1) * 128] = wide[i % 2, pl.ds(part, depth, stride=parts), :].astype(BF)
        if i == 0:
            tok_copy.wait()
        add = nn(tok_ref[:, i * depth : (i + 1) * depth], wflat_ref[rows, :])
        if i == 0:
            proj_ref[...] = add
        else:
            proj_ref[...] += add
    sw_copy.wait()
    swide[...] = jnp.zeros_like(swide)
    for level in range(sw_ref.shape[0]):
        swide[pl.ds(level * heads, heads), :] = sw_ref[level].astype(F32)
    swt = swide[...].astype(BF)
    swt_ref[...] = swt
    gate_ref[...] = nt(tok_ref[...], swt)


def project(tokens, qkv_weight, small_weight):
    rows, width = tokens.shape
    heads = qkv_weight.shape[2]
    extra = small_weight.shape[2]
    parts = 3 * heads
    depth = 512
    steps = width // depth
    return pl.pallas_call(
        functools.partial(proj_kernel, heads, depth),
        in_specs=[pl.BlockSpec(memory_space=pltpu.HBM)] * 3,
        out_specs=[pl.BlockSpec(memory_space=VM)] * 4,
        out_shape=[
            jax.ShapeDtypeStruct((rows, parts * 128), F32),
            jax.ShapeDtypeStruct((rows, heads * LANES), F32),
            jax.ShapeDtypeStruct((width, parts * 128), BF),
            jax.ShapeDtypeStruct((heads * LANES, width), BF),
        ],
        scratch_shapes=[
            VM((rows, width), BF), VM((steps, depth * parts, 128), BF), VM((extra, heads, width), BF),
            VM((2, depth * parts, 128), F32), VM((heads * LANES, width), F32), pltpu.SemaphoreType.DMA((steps + 2,)),
        ],
        compiler_params=pltpu.CompilerParams(vmem_limit_bytes=LIMIT["project"] * 2**20),
        name="project",
    )(tokens, qkv_weight.reshape(width * parts, 128), jnp.transpose(small_weight, (2, 1, 0)))


def unit(values):
    scale = lax.rsqrt(jnp.sum(values * values, -1, keepdims=True) + 1e-06)
    return values * scale, scale


def running_log(gate, rate, n):
    row, lane = iotas(n, n)
    lower = jnp.where(row >= lane, 1.0, 0.0).astype(F32)
    return lax.dot_general(
        lower, -rate * sigmoid(gate), (((1,), (0,)), ((), ())),
        precision=lax.Precision.HIGHEST, preferred_element_type=F32,
    )


def mask_rows(n, masks):
    row, lane = iotas(n, n)
    cross = jnp.bitwise_xor(row, lane)
    for k in range(masks.shape[0]):
        masks[k] = jnp.where(jnp.right_shift(cross, k) == 1, 1.0, 0.0).astype(BF)


def local_kernel(heads, levels, group, param_ref, proj_ref, gate_ref, au_ref, e_ref, lp_ref, t_ref, m_ref,
                 nk_ref, core_ref, qh_ref, clog_ref, masks, low):
    n = proj_ref.shape[0]
    gate = gate_ref[...]
    rate, bias = head_rows(param_ref, heads, n)
    clog = running_log(gate, rate, n)
    clog_ref[...] = clog
    clog_t = clog.T
    beta_all = sigmoid(gate + bias)
    lam_all = softplus(gate)
    mask_rows(n, masks)
    row, lane = iotas(n, n)
    cross = jnp.bitwise_xor(row, lane)
    incl = row >= lane
    strict = row > lane
    half = n // 2
    for first in range(0, heads, group):
        hs = range(first, first + group)
        keep = {}
        tb = {}
        score = {}
        for h in hs:
            q, _ = unit(proj_ref[:, h * 128 : (h + 1) * 128])
            k, _ = unit(proj_ref[:, (heads + h) * 128 : (heads + h + 1) * 128])
            v = proj_ref[:, (2 * heads + h) * 128 : (2 * heads + h + 1) * 128]
            qb, kb = q.astype(BF), k.astype(BF)
            beta = col(beta_all, lane_of(h, levels + 1, heads))
            cc = col(clog, lane_of(h, levels, heads))
            at = lane_of(h, levels, heads)
            end = clog_t[at : at + 1, n - 1 : n]
            crow = clog_t[at : at + 1, :]
            e = jnp.where(incl, jnp.exp(cc - crow), 0.0)
            s = (nt(qb, kb) * e).astype(BF)
            lp = jnp.where(strict, nt(kb, kb) * e, 0.0)
            lo = (lp * beta).astype(BF)
            e_ref[h] = e.astype(BF)
            score[h] = s
            lp_ref[h] = lp.astype(BF)
            low[h % group] = lo
            tb[h] = jnp.where(row == lane, 1.0, 0.0).astype(BF) - lo * masks[0]
            grow = jnp.exp(cc)
            keep[h] = (grow * q, (v * beta).astype(BF), ((beta * grow) * k).astype(BF),
                       (jnp.exp(end - cc) * k).astype(BF), end)
        for level in range(1, masks.shape[0]):
            for h in hs:
                w = nn(low[h % group] * masks[level], tb[h]).astype(BF)
                tb[h] = tb[h] - nn(tb[h], w).astype(BF)
        for h in hs:
            gq, vb, kbg, tk, end = keep[h]
            t_ref[h] = tb[h]
            m = nn(score[h], tb[h])
            mb = m.astype(BF)
            m_ref[h] = mb
            mix = nn(tb[h], jnp.concatenate([vb, kbg], 1)).astype(BF)
            nk_ref[h] = mix
            au = tn(mix, tk)
            r2, l2 = iotas(128, 128)
            au_ref[h, 0:128] = au[0:128].astype(BF)
            au_ref[h, 128:256] = (jnp.where(r2 == l2, jnp.exp(end), 0.0) - au[128:256]).astype(BF)
            lam = jnp.where(cross < 64, col(lam_all, lane_of(h, 0, heads)),
                            jnp.where(cross < 128, col(lam_all, lane_of(h, 1, heads)), col(lam_all, lane_of(h, 2, heads))))
            core_ref[h] = nn((m * lam).astype(BF), vb)
            qh_ref[h] = (gq - nn(mb, kbg)).astype(BF)


def local_forward(head_param, proj, gate, levels):
    rows = proj.shape[0]
    heads = head_param.shape[1]
    group = 4
    square = jax.ShapeDtypeStruct((heads, rows, rows), BF)
    bits = rows.bit_length() - 1
    return pl.pallas_call(
        functools.partial(local_kernel, heads, levels, group),
        in_specs=[pl.BlockSpec(memory_space=pltpu.SMEM), pl.BlockSpec(memory_space=VM), pl.BlockSpec(memory_space=VM)],
        out_specs=[pl.BlockSpec(memory_space=VM)] * 9,
        out_shape=[
            jax.ShapeDtypeStruct((heads, 256, 128), BF),
            square, square, square, square,
            jax.ShapeDtypeStruct((heads, rows, 256), BF),
            jax.ShapeDtypeStruct((heads, rows, 128), F32),
            jax.ShapeDtypeStruct((heads, rows, 128), BF),
            jax.ShapeDtypeStruct((rows, heads * LANES), F32),
        ],
        scratch_shapes=[VM((bits, rows, rows), BF), VM((group, rows, rows), BF)],
        compiler_params=pltpu.CompilerParams(vmem_limit_bytes=LIMIT["local"] * 2**20),
        name="local_forward",
    )(head_param, proj, gate)


def out_kernel(heads, levels, far, near, gate_ref, core_ref, qh_ref, x_ref, gain_ref, gn_ref,
               normed_ref, g_ref, dqh_ref, gx_ref, dlam_ref):
    n = gate_ref.shape[0]
    lam_all = softplus(gate_ref[...])
    lane = lax.broadcasted_iota(jnp.int32, (n, heads * LANES), 1)
    gain = gain_ref[...]
    dlam = jnp.zeros((n, heads * LANES), F32)
    for h in range(heads):
        qh = qh_ref[h]
        x = x_ref[h]
        w = nt(qh, x)
        core = core_ref[h]
        fw = [col(lam_all, lane_of(h, near + j, heads)) for j in range(far)]
        for j in range(far):
            core = core + fw[j] * w[:, j * 128 : (j + 1) * 128]
        rs = lax.rsqrt(jnp.mean(core * core, -1, keepdims=True) + 1e-06)
        unit_core = core * rs
        normed_ref[:, h * 128 : (h + 1) * 128] = (unit_core * gain).astype(BF)
        gy = gn_ref[:, h * 128 : (h + 1) * 128] * gain
        g = rs * (gy - unit_core * jnp.mean(gy * unit_core, -1, keepdims=True))
        g_ref[h] = g.astype(BF)
        fg = jnp.concatenate([(fw[j] * g).astype(BF) for j in range(far)], 1)
        for j in range(far):
            here = jnp.sum(g * w[:, j * 128 : (j + 1) * 128], -1, keepdims=True)
            dlam = jnp.where(lane == lane_of(h, near + j, heads), here, dlam)
        dqh_ref[h] = nn(fg, x).astype(BF)
        gx_ref[h] = tn(fg, qh).astype(BF)
    dlam_ref[...] = dlam


def out_stage(gate, core, qh, x, gain, grad_normed, levels, far, near):
    rows = gate.shape[0]
    heads = core.shape[0]
    return pl.pallas_call(
        functools.partial(out_kernel, heads, levels, far, near),
        in_specs=[pl.BlockSpec(memory_space=VM)] * 6,
        out_specs=[pl.BlockSpec(memory_space=VM)] * 5,
        out_shape=[
            jax.ShapeDtypeStruct((rows, heads * 128), BF),
            jax.ShapeDtypeStruct((heads, rows, 128), BF),
            jax.ShapeDtypeStruct((heads, rows, 128), BF),
            jax.ShapeDtypeStruct((heads, far * 128, 128), BF),
            jax.ShapeDtypeStruct((rows, heads * LANES), F32),
        ],
        compiler_params=pltpu.CompilerParams(vmem_limit_bytes=LIMIT["out"] * 2**20),
        name="out_stage",
    )(gate, core, qh, x, gain, grad_normed)


def back_kernel(heads, levels, group, param_ref, proj_ref, gate_ref, clog_ref, e_ref, lp_ref, t_ref, m_ref,
                nk_ref, g_ref, dqh_ref, dau_ref, dlam_ref, layer_ref, dproj_ref, dgate_ref, out_ref):
    n = proj_ref.shape[0]
    gate = gate_ref[...]
    rate, bias = head_rows(param_ref, heads, n)
    clog = clog_ref[...]
    beta_all = sigmoid(gate + bias)
    sig_all = sigmoid(gate)
    lam_all = softplus(gate)
    row, lane = iotas(n, n)
    cross = jnp.bitwise_xor(row, lane)
    strict = row > lane
    eye = jnp.where(row == lane, 1.0, 0.0).astype(BF)

    def tq(a, b):
        return nn(nt(eye, a).astype(BF), b)

    out_ref[...] = layer_ref[...]
    wide = lax.broadcasted_iota(jnp.int32, (n, heads * LANES), 1)
    dlam = dlam_ref[...]
    source, target = iotas(n, heads * LANES)

    def pick_level(block, h):
        apart = jnp.bitwise_xor(jnp.right_shift(source, 6), block)
        near_level = jnp.where(apart == 0, 0, jnp.where(apart == 1, 1, 2))
        return jnp.where(target == near_level * heads + h, 1.0, 0.0).astype(BF)

    dlog = jnp.zeros((n, heads * LANES), F32)
    dbeta_all = jnp.zeros((n, heads * LANES), F32)
    last = lax.broadcasted_iota(jnp.int32, (n, 1), 0) == n - 1
    out = [None] * (3 * heads)
    for first in range(0, heads, group):
        for h in range(first, first + group):
            q, rq = unit(proj_ref[:, h * 128 : (h + 1) * 128])
            k, rk = unit(proj_ref[:, (heads + h) * 128 : (heads + h + 1) * 128])
            v = proj_ref[:, (2 * heads + h) * 128 : (2 * heads + h + 1) * 128]
            qb, kb = q.astype(BF), k.astype(BF)
            beta = col(beta_all, lane_of(h, levels + 1, heads))
            cc = col(clog, lane_of(h, levels, heads))
            at = lane_of(h, levels, heads)
            end = clog[n - 1 : n, at : at + 1]
            grow = jnp.exp(cc)
            tail = jnp.exp(end - cc)
            vb = (v * beta).astype(BF)
            kbg = ((beta * grow) * k).astype(BF)
            tk = (tail * k).astype(BF)
            g, dqh = g_ref[h], dqh_ref[h]
            mb, tb, mix = m_ref[h], t_ref[h], nk_ref[h]
            m = mb.astype(F32)
            lam = jnp.where(cross < 64, col(lam_all, lane_of(h, 0, heads)),
                            jnp.where(cross < 128, col(lam_all, lane_of(h, 1, heads)), col(lam_all, lane_of(h, 2, heads))))
            dmw = nt(g, vb)
            prod = m * dmw
            pb = prod.astype(BF)
            dlam = dlam + jnp.concatenate(
                [nn(pb[b * 64 : (b + 1) * 64], pick_level(b, h)) for b in range(n // 64)], 0)
            mw = (m * lam).astype(BF)
            dm = (lam * dmw - nt(dqh, kbg)).astype(BF)
            dau = dau_ref[h]
            du, da = dau[0:128], dau[128:256]
            dnv = nt(tk, du)
            dkt = -nt(tk, da)
            dtk = nn(mix[:, 0:128], du) - nn(mix[:, 128:256], da)
            dmix = jnp.concatenate([dnv.astype(BF), dkt.astype(BF)], 1)
            back = tq(tb, dmix)
            dvb2, dkbg2 = back[:, 0:128], back[:, 128:256]
            dst = nt(dm, tb)
            dstb = dst.astype(BF)
            dvb = tq(mw, g) + dvb2
            both = tq(mb, jnp.concatenate([dqh, dstb], 1))
            dkbg = dkbg2 - both[:, 0:128]
            dlow = both[:, 128:] + nt(back.astype(BF), mix)
            dlow = jnp.where(strict, -dlow, 0.0)
            e = e_ref[h].astype(F32)
            dp = (dst * e).astype(BF)
            lp = lp_ref[h].astype(F32)
            dbeta = jnp.sum(dlow * lp, -1, keepdims=True)
            dkk = (dlow * (beta * e)).astype(BF)
            dq1 = nn(dp, kb)
            dk1 = tq(dp, qb)
            dk2 = nn(dkk, kb)
            dk3 = tq(dkk, kb)
            qr, kr = qb.astype(F32), kb.astype(F32)
            dqf, dtf, dkf = dqh.astype(F32), dtk, dkbg
            gq = jnp.sum(dqf * q, -1, keepdims=True)
            kk = jnp.sum(dkf * k, -1, keepdims=True)
            dtail = jnp.sum(dtf * k, -1, keepdims=True) * tail
            dc = jnp.sum(qr * dq1 + kr * (dk2 - dk1 - dk3), -1, keepdims=True)
            dc = dc + grow * (gq + beta * kk) - dtail
            r2, l2 = iotas(128, 128)
            trace = jnp.sum(jnp.where(r2 == l2, da.astype(F32), 0.0), keepdims=True)
            dend = jnp.sum(dtail, keepdims=True) + jnp.exp(end) * trace
            dc = dc + jnp.where(last, dend, 0.0)
            dbeta = dbeta + jnp.sum(dvb * v, -1, keepdims=True) + grow * kk
            dq = dq1 + grow * dqf
            dk = dk1 + dk2 + dk3 + (beta * grow) * dkf + tail * dtf
            dv = beta * dvb
            out[h] = (rq * (dq - q * jnp.sum(q * dq, -1, keepdims=True))).astype(BF)
            out[heads + h] = (rk * (dk - k * jnp.sum(k * dk, -1, keepdims=True))).astype(BF)
            out[2 * heads + h] = dv.astype(BF)
            dlog = jnp.where(wide == lane_of(h, levels, heads), dc, dlog)
            dbeta_all = jnp.where(wide == lane_of(h, levels + 1, heads), dbeta, dbeta_all)
    upper = jnp.where(lane >= row, 1.0, 0.0).astype(F32)
    dstep = lax.dot_general(upper, dlog, (((1,), (0,)), ((), ())),
                            precision=lax.Precision.HIGHEST, preferred_element_type=F32)
    dgate = dlam * sig_all - rate * sig_all * (1.0 - sig_all) * dstep + beta_all * (1.0 - beta_all) * dbeta_all
    dgate_ref[...] = dgate.astype(BF)
    for j, grad in enumerate(out):
        dproj_ref[:, j * 128 : (j + 1) * 128] = grad


def back_stage(head_param, proj, gate, clog, saved, g, dqh, dau, dlam, layer, levels):
    rows = proj.shape[0]
    heads = head_param.shape[1]
    return pl.pallas_call(
        functools.partial(back_kernel, heads, levels, 1),
        in_specs=[pl.BlockSpec(memory_space=pltpu.SMEM)] + [pl.BlockSpec(memory_space=VM)] * 13,
        out_specs=[pl.BlockSpec(memory_space=VM)] * 3,
        out_shape=[jax.ShapeDtypeStruct((rows, 3 * heads * 128), BF), jax.ShapeDtypeStruct((rows, heads * LANES), BF),
                   jax.ShapeDtypeStruct(layer.shape, BF)],
        compiler_params=pltpu.CompilerParams(vmem_limit_bytes=LIMIT["back"] * 2**20),
        name="back_stage",
    )(head_param, proj, gate, clog, *saved, g, dqh, dau, dlam, layer)


MESH = pl.DeviceIdType.MESH
RING = 4


def place():
    ctx = lax.axis_index("ctx")
    return lax.div(ctx, 2 * RING), lax.rem(lax.div(ctx, 2), RING), lax.rem(ctx, 2)


def at_ctx(x, y, core):
    return {"ctx": (x * RING + y) * 2 + core}


def around(index, step):
    return lax.rem(index + step + RING, RING)


def greet(peers):
    barrier = pltpu.get_barrier_semaphore()
    for peer in peers:
        pl.semaphore_signal(barrier, inc=1, device_id=peer, device_id_type=MESH)
    pl.semaphore_wait(barrier, len(peers))


def remote(src, dst, send, recv, index, peer):
    return pltpu.make_async_remote_copy(
        src_ref=src, dst_ref=dst, send_sem=send.at[index], recv_sem=recv.at[index],
        device_id=peer, device_id_type=MESH)


class Ring:
    def __init__(self, buf, i, send, recv, base, right, left, low, middle):
        rows = buf.shape[2]
        first, second, whole = pl.ds(low, middle - low), pl.ds(middle, rows - middle), pl.ds(0, middle)

        def copy(index, slot, to, part, peer):
            return remote(buf.at[slot, i, part], buf.at[to, i, part], send, recv, base + index, peer)

        self.near = [copy(0, 0, 1, first, right), copy(1, 0, 3, second, left),
                     copy(2, 0, 1, second, right), copy(3, 0, 3, whole, left)]
        self.far = [copy(4, 1, 2, first, right), copy(5, 3, 2, second, left)]
        for one in self.near:
            one.start()

    def relay(self):
        for near, far in zip(self.near, self.far):
            near.wait_recv()
            far.start()

    def arrive(self):
        for one in self.near[2:] + self.far:
            one.wait_recv()

    def leave(self):
        for one in self.near + self.far:
            one.wait_send()


def flag(cond):
    return jnp.where(cond, 1.0, 0.0).astype(F32)


def gather_kernel(au_ref, gout_ref, ow_ref, x_ref, cores_ref, ys_ref, xs_ref, gn_ref, cores, ys, xs, share, send, recv, local):
    x, y, core = place()
    partner = at_ctx(x, y, 1 - core)
    y_right, y_left = at_ctx(x, around(y, 1), core), at_ctx(x, around(y, -1), core)
    x_right, x_left = at_ctx(around(x, 1), y, core), at_ctx(around(x, -1), y, core)
    greet((partner, y_right, y_left, x_right, x_left))
    first = core * 2
    mine, yours = pl.ds(first, 2), pl.ds(2 - first, 2)
    out = [remote(au_ref.at[part], cores.at[core, part], send, recv, k, partner) for k, part in enumerate((yours, mine))]
    take = [remote(au_ref.at[part], cores.at[1 - core, part], send, recv, k, partner) for k, part in enumerate((mine, yours))]
    for one in out:
        one.start()
    keep = pltpu.make_async_copy(au_ref, cores.at[core], local.at[0])
    keep.start()
    gn_ref[...] = nt(gout_ref[...], ow_ref[...])
    eye_r, eye_c = iotas(128, 128)
    eye = jnp.where(eye_r == eye_c, 1.0, 0.0).astype(F32)

    def joined(below, above):
        moved = nn(below, above[128:256])
        return jnp.concatenate([moved[0:128] + above[0:128].astype(F32), moved[128:256]], 0)

    keep.wait()
    take[0].wait_recv()
    ring = []
    for i in range(2):
        ys[0, i] = joined(cores[0, first + i], cores[1, first + i]).astype(BF)
        ring.append(Ring(ys, i, send, recv, 2 + 6 * i, y_right, y_left, 0, 128))
    for i in range(2):
        ring[i].relay()
    prefix = [None, None]
    cols = []
    for i in range(2):
        ring[i].arrive()
        at = [ys[around(y, -k), i] for k in range(RING)]
        s1 = joined(at[0], at[1])
        s2 = joined(s1.astype(BF), at[2])
        s3 = joined(s2.astype(BF), at[3])
        xs[0, i] = s3.astype(BF)
        cols.append(Ring(xs, i, send, recv, 14 + 6 * i, x_right, x_left, 0, 128))
        x1 = flag(lax.rem(y, 2) == 1) * ys[1, i, 0:128].astype(F32)
        s1u = s1[0:128]
        x2 = flag(y == 2) * s1u + flag(y == 3) * nn(s1u.astype(BF), at[2][128:256])
        share[first + i, 0:128] = x1.astype(BF)
        share[first + i, 128:256] = x2.astype(BF)
        prefix[i] = (flag(y == 0) * eye + flag(y == 1) * at[0][128:256].astype(F32)
                     + flag(y == 2) * s1[128:256] + flag(y == 3) * s2[128:256]).astype(BF)
    for i in range(2):
        cols[i].relay()
    give, got = [], []
    for i in range(2):
        cols[i].arrive()
        at = [xs[around(x, -k), i] for k in range(RING)]
        r1 = nn(at[0][0:128], at[1][128:256]) + at[1][0:128].astype(F32)
        x3 = flag(lax.rem(x, 2) == 1) * xs[1, i, 0:128].astype(F32)
        x4 = flag(x == 2) * r1 + flag(x == 3) * nn(r1.astype(BF), at[2][128:256])
        both = jnp.concatenate([x3.astype(BF), x4.astype(BF)], 0)
        share[first + i, 256:512] = nn(both, prefix[i]).astype(BF)
        give.append(remote(share.at[first + i], share.at[first + i], send, recv, 26 + i, partner))
        got.append(remote(share.at[2 - first + i], share.at[2 - first + i], send, recv, 26 + i, partner))
        give[i].start()
    upper = flag(core == 1)
    take[1].wait_recv()
    step = []
    for h in range(4):
        below = cores[0, h]
        x_ref[h, 0:128] = (upper * below[0:128].astype(F32)).astype(BF)
        step.append((upper * below[128:256].astype(F32) + (1.0 - upper) * eye).astype(BF))
    cores_ref[...] = cores[...]
    ys_ref[...] = ys[...]
    xs_ref[...] = xs[...]
    for i in range(2):
        x_ref[first + i, 128:640] = nn(share[first + i], jnp.where(core == 0, step[i], step[2 + i])).astype(BF)
    for i in range(2):
        got[i].wait_recv()
        x_ref[2 - first + i, 128:640] = nn(share[2 - first + i], jnp.where(core == 0, step[2 + i], step[i])).astype(BF)
    for one in out + give:
        one.wait_send()
    for one in ring + cols:
        one.leave()


def gather_states(au, grad_out, out_weight):
    heads = au.shape[0]
    cores = ((2, heads, 256, 128), BF)
    ring = ((RING, 2, 256, 128), BF)
    return pl.pallas_call(
        gather_kernel,
        in_specs=[pl.BlockSpec(memory_space=VM)] * 3,
        out_specs=[pl.BlockSpec(memory_space=VM)] * 5,
        out_shape=[jax.ShapeDtypeStruct((heads, 640, 128), BF)] + [jax.ShapeDtypeStruct(*s) for s in (cores, ring, ring)]
        + [jax.ShapeDtypeStruct((grad_out.shape[0], heads * 128), F32)],
        scratch_shapes=[VM(*cores), VM(*ring), VM(*ring), VM((heads, 512, 128), BF),
                        pltpu.SemaphoreType.DMA((28,)), pltpu.SemaphoreType.DMA((28,)), pltpu.SemaphoreType.DMA((1,))],
        compiler_params=pltpu.CompilerParams(
            collective_id=1, has_side_effects=True, vmem_limit_bytes=LIMIT["gather"] * 2**20),
        name="gather_states",
    )(au, grad_out, out_weight)


def return_kernel(groups, gx_ref, x_ref, cores_ref, ys_ref, xs_ref, normed_ref, ow_ref, dau_ref, layer_ref,
                  part_ref, pair, ys, xs, share, chunks, send, recv, local, zsend, zrecv):
    x, y, core = place()
    z = lax.axis_index("head")
    partner = at_ctx(x, y, 1 - core)
    y_right, y_left = at_ctx(x, around(y, 1), core), at_ctx(x, around(y, -1), core)
    x_right, x_left = at_ctx(around(x, 1), y, core), at_ctx(around(x, -1), y, core)
    across = [{"head": lax.rem(z + k, groups)} for k in range(1, groups)]
    greet([partner, y_right, y_left, x_right, x_left] + across)
    first = core * 2
    mine, yours = pl.ds(first, 2), pl.ds(2 - first, 2)
    out = [remote(gx_ref.at[part], pair.at[core, part], send, recv, k, partner) for k, part in enumerate((yours, mine))]
    take = [remote(gx_ref.at[part], pair.at[1 - core, part], send, recv, k, partner) for k, part in enumerate((mine, yours))]
    for one in out:
        one.start()
    keep = pltpu.make_async_copy(gx_ref, pair.at[core], local.at[0])
    keep.start()
    wide = part_ref.shape[2]
    for j in range(groups):
        part_ref[j] = nn(normed_ref[...], ow_ref[:, j * wide : (j + 1) * wide]).astype(BF)
    spread = []
    for k in range(1, groups):
        to = lax.rem(z + k, groups)
        spread.append(remote(part_ref.at[to], chunks.at[k - 1], zsend, zrecv, k - 1, across[k - 1]))
        spread[-1].start()
    upper = flag(core == 1)
    bits = [upper, flag(lax.rem(y, 2) == 1), flag(y >= 2), flag(lax.rem(x, 2) == 1), flag(x >= 2)]
    eye_r, eye_c = iotas(128, 128)
    eye = jnp.where(eye_r == eye_c, 1.0, 0.0).astype(F32)
    after = [None, None]
    for i in range(2):
        at = [ys_ref[around(y, -k), i, 128:256] for k in range(RING)]
        q1 = nn(at[2], at[3])
        q0 = nn(at[1], q1.astype(BF))
        after[i] = (flag(y == 3) * eye + flag(y == 2) * at[3].astype(F32) + flag(y == 1) * q1 + flag(y == 0) * q0).astype(BF)
    keep.wait()
    take[0].wait_recv()
    ring = []
    for i in range(2):
        total = pair[0, first + i, 128:640].astype(F32) + nt(pair[1, first + i, 128:640], cores_ref[0, first + i, 128:256])
        for k in range(4):
            ys[0, i, k * 128 : (k + 1) * 128] = (bits[k + 1] * total[k * 128 : (k + 1) * 128]).astype(BF)
        ring.append(Ring(ys, i, send, recv, 2 + 6 * i, y_right, y_left, 128, 320))
    for i in range(2):
        ring[i].relay()
    held = [None, None]
    cols = []
    for i in range(2):
        ring[i].arrive()
        trans = [ys_ref[around(y, -k), i, 128:256] for k in range(RING)]
        at = [ys[around(y, -k), i, 128:512] for k in range(RING)]
        h1 = nt(at[3], trans[2]) + at[2].astype(F32)
        h0 = nt(h1.astype(BF), trans[1]) + at[1].astype(F32)
        column = nt(h0[128:384].astype(BF), trans[0]) + at[0][128:384].astype(F32)
        xs[0, i] = column.astype(BF)
        cols.append(Ring(xs, i, send, recv, 14 + 6 * i, x_right, x_left, 0, 128))
        held[i] = flag(y == 2) * at[3].astype(F32) + flag(y == 1) * h1 + flag(y == 0) * h0
        share[first + i, 0:128] = ((1.0 - bits[1]) * ys[3, i, 0:128].astype(F32)).astype(BF)
        share[first + i, 128:256] = held[i][0:128].astype(BF)
    for i in range(2):
        cols[i].relay()
    give, got = [], []
    for i in range(2):
        cols[i].arrive()
        trans = [xs_ref[around(x, -k), i, 128:256] for k in range(RING)]
        at = [xs[around(x, -k), i, 128:256] for k in range(RING)]
        h1 = nt(at[3], trans[2]) + at[2].astype(F32)
        h0 = nt(h1.astype(BF), trans[1]) + at[1].astype(F32)
        v4 = flag(x == 2) * at[3].astype(F32) + flag(x == 1) * h1 + flag(x == 0) * h0
        v3 = (1.0 - bits[3]) * xs[3, i, 0:128].astype(F32)
        both = jnp.concatenate([v3.astype(BF), v4.astype(BF)], 0)
        share[first + i, 256:512] = (held[i][128:384] + nt(both, after[i])).astype(BF)
        give.append(remote(share.at[first + i], share.at[first + i], send, recv, 26 + i, partner))
        got.append(remote(share.at[2 - first + i], share.at[2 - first + i], send, recv, 26 + i, partner))
        give[i].start()
    take[1].wait_recv()

    def finish(h):
        move = (upper * eye + (1.0 - upper) * cores_ref[1, h, 128:256].astype(F32)).astype(BF)
        v = nt(share[h], move)
        parts = [(1.0 - upper) * pair[1, h, 0:128].astype(F32)]
        for k in range(4):
            keep_it = (1.0 - upper) * bits[k + 1]
            parts.append(v[k * 128 : (k + 1) * 128] + keep_it * pair[1, h, (k + 1) * 128 : (k + 2) * 128].astype(F32))
        so_far = jnp.zeros((128, 128), F32)
        du = jnp.zeros((128, 128), F32)
        states = []
        for k in range(5):
            state = x_ref[h, k * 128 : (k + 1) * 128].astype(F32)
            states.append((bits[k] * state + (1.0 - bits[k]) * so_far).astype(BF))
            so_far = so_far + state
            du = du + (1.0 - bits[k]) * parts[k]
        da = tn(jnp.concatenate(states, 0), jnp.concatenate([p.astype(BF) for p in parts], 0))
        dau_ref[h, 0:128] = du.astype(BF)
        dau_ref[h, 128:256] = da.astype(BF)

    for i in range(2):
        finish(first + i)
    for i in range(2):
        got[i].wait_recv()
        finish(2 - first + i)
    total = part_ref[z].astype(F32)
    for copy in spread:
        copy.wait_recv()
    for k in range(groups - 1):
        total = total + chunks[k].astype(F32)
    layer_ref[...] = total.astype(BF)
    for one in out + give + spread:
        one.wait_send()
    for one in ring + cols:
        one.leave()


def return_grads(gx, x, cores, ys, xs, normed, out_weight, groups):
    heads = gx.shape[0]
    rows, wide = normed.shape[0], out_weight.shape[1] // groups
    ring = (RING, 2)
    return pl.pallas_call(
        functools.partial(return_kernel, groups),
        in_specs=[pl.BlockSpec(memory_space=VM)] * 7,
        out_specs=[pl.BlockSpec(memory_space=VM)] * 2,
        out_shape=[jax.ShapeDtypeStruct((heads, 256, 128), BF), jax.ShapeDtypeStruct((rows, wide), BF)],
        scratch_shapes=[VM((groups, rows, wide), BF), VM((2, heads, 640, 128), BF), VM(ring + (512, 128), BF), VM(ring + (256, 128), BF),
                        VM((heads, 512, 128), BF), VM((3, rows, wide), BF),
                        pltpu.SemaphoreType.DMA((28,)), pltpu.SemaphoreType.DMA((28,)), pltpu.SemaphoreType.DMA((1,)),
                        pltpu.SemaphoreType.DMA((3,)), pltpu.SemaphoreType.DMA((3,))],
        compiler_params=pltpu.CompilerParams(
            collective_id=2, has_side_effects=True, vmem_limit_bytes=LIMIT["return"] * 2**20),
        name="return_grads",
    )(gx, x, cores, ys, xs, normed, out_weight)


def last_kernel(groups, dproj_ref, dgate_ref, w_ref, sw_ref, out_ref, mine, relay, direct, extra, arrive, send, recv):
    rows, wide = out_ref.shape
    z = lax.axis_index("head")
    half = wide // 2
    right, left = {"head": lax.rem(z + 1, groups)}, {"head": lax.rem(z + groups - 1, groups)}
    greet((right, left))
    dproj, dgate = dproj_ref[...], dgate_ref[...]

    def product(step):
        chunk = lax.rem(z + step + groups, groups)
        at = pl.ds(pl.multiple_of(chunk * wide, wide), wide)
        return nt(dproj, w_ref[at, :]) + nn(dgate, sw_ref[:, at])

    far = product(2)
    relay[0] = far[:, :half].astype(BF)
    relay[1] = far[:, half:].astype(BF)
    far_right = remote(relay.at[0], arrive.at[0], send, recv, 0, right)
    far_left = remote(relay.at[1], arrive.at[1], send, recv, 1, left)
    far_right.start()
    far_left.start()
    to_right = product(1)
    direct[0] = to_right[:, half:].astype(BF)
    near_right = remote(direct.at[0], arrive.at[2], send, recv, 2, right)
    near_right.start()
    to_left = product(-1)
    direct[1] = to_left[:, :half].astype(BF)
    near_left = remote(direct.at[1], arrive.at[3], send, recv, 3, left)
    near_left.start()
    far_right.wait_recv()
    extra[0] = (to_right[:, :half] + arrive[0].astype(F32)).astype(BF)
    sum_right = remote(extra.at[0], arrive.at[4], send, recv, 4, right)
    sum_right.start()
    far_left.wait_recv()
    extra[1] = (to_left[:, half:] + arrive[1].astype(F32)).astype(BF)
    sum_left = remote(extra.at[1], arrive.at[5], send, recv, 5, left)
    sum_left.start()
    mine[...] = product(0)
    near_right.wait_recv()
    near_left.wait_recv()
    sum_right.wait_recv()
    sum_left.wait_recv()
    out_ref[:, :half] = (mine[:, :half] + arrive[4].astype(F32) + arrive[3].astype(F32)).astype(BF)
    out_ref[:, half:] = (mine[:, half:] + arrive[5].astype(F32) + arrive[2].astype(F32)).astype(BF)
    for copy in (far_right, far_left, near_right, near_left, sum_right, sum_left):
        copy.wait_send()


def last_stage(dproj, dgate, wflat, swt, groups):
    rows = dproj.shape[0]
    wide = wflat.shape[0] // groups
    half = (rows, wide // 2)
    return pl.pallas_call(
        functools.partial(last_kernel, groups),
        in_specs=[pl.BlockSpec(memory_space=VM)] * 4,
        out_specs=pl.BlockSpec(memory_space=VM),
        out_shape=jax.ShapeDtypeStruct((rows, wide), BF),
        scratch_shapes=[VM((rows, wide), F32), VM((2,) + half, BF), VM((2,) + half, BF), VM((2,) + half, BF),
                        VM((6,) + half, BF), pltpu.SemaphoreType.DMA((6,)), pltpu.SemaphoreType.DMA((6,))],
        compiler_params=pltpu.CompilerParams(
            collective_id=3, has_side_effects=True, vmem_limit_bytes=LIMIT["last"] * 2**20),
        name="last_stage",
    )(dproj, dgate, wflat, swt)


def on_device(tokens, qkv_weight, small_weight, head_param, norm_gain, out_weight, grad_out):
    rows, width = tokens.shape
    heads = qkv_weight.shape[2]
    levels = small_weight.shape[2] - 2
    near = (rows // 64).bit_length()
    far = lax.axis_size("ctx").bit_length() - 1
    groups = lax.axis_size("head")
    rates = head_param.T
    proj, gate, wflat, swt = project(tokens, qkv_weight, small_weight)
    au, *saved, core, qh, clog = local_forward(rates, proj, gate, levels)
    flat_out = out_weight.reshape(heads * 128, width)
    x, cores, ys, xs, grad_normed = gather_states(au, grad_out, flat_out)
    normed, g, dqh, gx, dlam = out_stage(gate, core, qh, x, norm_gain.reshape(1, -1), grad_normed, levels, far, near)
    dau, layer = return_grads(gx, x, cores, ys, xs, normed, flat_out, groups)
    dproj, dgate, layer_out = back_stage(rates, proj, gate, clog, saved, g, dqh, dau, dlam, layer, levels)
    grad_tokens = last_stage(dproj, dgate, wflat, swt, groups)
    return (layer_out, grad_tokens)


def solution(mesh):
    placed = (
        P("ctx", None),
        P(None, None, "head", None),
        P(None, "head", None),
        P("head", None),
        P(),
        P("head", None, None),
        P("ctx", None),
    )
    return jax.shard_map(
        on_device,
        mesh=mesh,
        in_specs=placed,
        out_specs=(P("ctx", "head"), P("ctx", "head")),
        check_vma=False,
    )
```

```python
import functools

import jax
import jax.numpy as jnp
from jax import lax
from jax.experimental import pallas as pl
from jax.experimental.pallas import tpu as pltpu
from jax.sharding import PartitionSpec as P

BF = jnp.bfloat16
F32 = jnp.float32
LANES = 32
LIMIT = {"project": 44, "local": 24, "gather": 16, "out": 16, "return": 20, "back": 24, "last": 24}


def lane_of(h, level, heads):
    return level * heads + h
VM = pltpu.VMEM


def nn(a, b):
    return lax.dot_general(a, b, (((1,), (0,)), ((), ())), preferred_element_type=F32)


def nt(a, b):
    return lax.dot_general(a, b, (((1,), (1,)), ((), ())), preferred_element_type=F32)


def tn(a, b):
    return lax.dot_general(a, b, (((0,), (0,)), ((), ())), preferred_element_type=F32)


def sigmoid(x):
    return 1.0 / (1.0 + jnp.exp(-x))


def softplus(x):
    return jnp.maximum(x, 0.0) + jnp.log(1.0 + jnp.exp(-jnp.abs(x)))


def iotas(n, m):
    return lax.broadcasted_iota(jnp.int32, (n, m), 0), lax.broadcasted_iota(jnp.int32, (n, m), 1)


def col(array, lane):
    return array[:, lane : lane + 1]


def head_rows(param_ref, heads, rows):
    lane = lax.broadcasted_iota(jnp.int32, (rows, heads * LANES), 1)
    rate = jnp.zeros((rows, heads * LANES), F32)
    bias = jnp.zeros((rows, heads * LANES), F32)
    for h in range(heads):
        here = lane % heads == h
        rate = jnp.where(here, param_ref[0, h], rate)
        bias = jnp.where(here, param_ref[1, h], bias)
    return rate, bias


def proj_kernel(heads, depth, tok_hbm, w_hbm, sw_hbm, proj_ref, gate_ref, wflat_ref, swt_ref, tok_ref, w_ref, sw_ref, wide, swide, sems):
    parts = 3 * heads
    steps = w_ref.shape[0]
    span = depth * parts
    tok_copy = pltpu.make_async_copy(tok_hbm, tok_ref, sems.at[steps])
    sw_copy = pltpu.make_async_copy(sw_hbm, sw_ref, sems.at[steps + 1])
    copies = [pltpu.make_async_copy(w_hbm.at[pl.ds(i * span, span)], w_ref.at[i], sems.at[i]) for i in range(steps)]
    copies[0].start()
    tok_copy.start()
    for copy in copies[1:]:
        copy.start()
    sw_copy.start()
    for i in range(steps):
        copies[i].wait()
        rows = pl.ds(i * depth, depth)
        wide[i % 2] = w_ref[i].astype(F32)
        for part in range(parts):
            wflat_ref[rows, part * 128 : (part + 1) * 128] = wide[i % 2, pl.ds(part, depth, stride=parts), :].astype(BF)
        if i == 0:
            tok_copy.wait()
        if i == steps // 2 - 1:
            proj_ref[...] = nn(tok_ref[:, : (i + 1) * depth], wflat_ref[: (i + 1) * depth, :])
        if i == steps - 1:
            proj_ref[...] += nn(tok_ref[:, steps // 2 * depth :], wflat_ref[steps // 2 * depth :, :])
    sw_copy.wait()
    swide[...] = jnp.zeros_like(swide)
    for level in range(sw_ref.shape[0]):
        swide[pl.ds(level * heads, heads), :] = sw_ref[level].astype(F32)
    swt = swide[...].astype(BF)
    swt_ref[...] = swt
    gate_ref[...] = nt(tok_ref[...], swt)


def project(tokens, qkv_weight, small_weight):
    rows, width = tokens.shape
    heads = qkv_weight.shape[2]
    extra = small_weight.shape[2]
    parts = 3 * heads
    depth = 512
    steps = width // depth
    return pl.pallas_call(
        functools.partial(proj_kernel, heads, depth),
        in_specs=[pl.BlockSpec(memory_space=pltpu.HBM)] * 3,
        out_specs=[pl.BlockSpec(memory_space=VM)] * 4,
        out_shape=[
            jax.ShapeDtypeStruct((rows, parts * 128), F32),
            jax.ShapeDtypeStruct((rows, heads * LANES), F32),
            jax.ShapeDtypeStruct((width, parts * 128), BF),
            jax.ShapeDtypeStruct((heads * LANES, width), BF),
        ],
        scratch_shapes=[
            VM((rows, width), BF), VM((steps, depth * parts, 128), BF), VM((extra, heads, width), BF),
            VM((2, depth * parts, 128), F32), VM((heads * LANES, width), F32), pltpu.SemaphoreType.DMA((steps + 2,)),
        ],
        compiler_params=pltpu.CompilerParams(vmem_limit_bytes=LIMIT["project"] * 2**20),
        name="project",
    )(*(pltpu.with_memory_space_constraint(part, pltpu.HBM) for part in (
        tokens, qkv_weight.reshape(width * parts, 128), jnp.transpose(small_weight, (2, 1, 0)))))


def unit(values):
    scale = lax.rsqrt(jnp.sum(values * values, -1, keepdims=True) + 1e-06)
    return values * scale, scale


def running_log(gate, rate, n):
    row, lane = iotas(n, n)
    lower = jnp.where(row >= lane, 1.0, 0.0).astype(F32)
    return lax.dot_general(
        lower, -rate * sigmoid(gate), (((1,), (0,)), ((), ())),
        precision=lax.Precision.HIGHEST, preferred_element_type=F32,
    )


def mask_rows(n, masks):
    row, lane = iotas(n, n)
    cross = jnp.bitwise_xor(row, lane)
    for k in range(masks.shape[0]):
        masks[k] = jnp.where(jnp.right_shift(cross, k) == 1, 1.0, 0.0).astype(BF)


def local_kernel(heads, levels, group, param_ref, proj_ref, gate_ref, au_ref, e_ref, lp_ref, t_ref, m_ref,
                 nk_ref, core_ref, qh_ref, clog_ref, masks, low):
    n = proj_ref.shape[0]
    gate = gate_ref[...]
    rate, bias = head_rows(param_ref, heads, n)
    clog = running_log(gate, rate, n)
    clog_ref[...] = clog
    clog_t = clog.T
    beta_all = sigmoid(gate + bias)
    lam_all = softplus(gate)
    half = n // 2
    mask_rows(half, masks)
    eye_row, eye_col = iotas(half, half)
    eye = jnp.where(eye_row == eye_col, 1.0, 0.0).astype(BF)
    row, lane = iotas(n, n)
    cross = jnp.bitwise_xor(row, lane)
    incl = row >= lane
    strict = row > lane
    half = n // 2
    for first in range(0, heads, group):
        hs = range(first, first + group)
        keep = {}
        tb = {}
        score = {}
        for h in hs:
            q, _ = unit(proj_ref[:, h * 128 : (h + 1) * 128])
            k, _ = unit(proj_ref[:, (heads + h) * 128 : (heads + h + 1) * 128])
            v = proj_ref[:, (2 * heads + h) * 128 : (2 * heads + h + 1) * 128]
            qb, kb = q.astype(BF), k.astype(BF)
            beta = col(beta_all, lane_of(h, levels + 1, heads))
            cc = col(clog, lane_of(h, levels, heads))
            at = lane_of(h, levels, heads)
            end = clog_t[at : at + 1, n - 1 : n]
            crow = clog_t[at : at + 1, :]
            e = jnp.where(incl, jnp.exp(cc - crow), 0.0)
            s = (nt(qb, kb) * e).astype(BF)
            lp = jnp.where(strict, nt(kb, kb) * e, 0.0)
            lo = (lp * beta).astype(BF)
            e_ref[h] = e.astype(BF)
            score[h] = s
            lp_ref[h] = lp.astype(BF)
            low[h % group] = lo
            for b in range(2):
                own = lo[b * half : (b + 1) * half, b * half : (b + 1) * half]
                tb[h, b] = eye - own * masks[0]
            grow = jnp.exp(cc)
            keep[h] = (grow * q, (v * beta).astype(BF), ((beta * grow) * k).astype(BF),
                       (jnp.exp(end - cc) * k).astype(BF), end)
        for level in range(1, masks.shape[0]):
            for h in hs:
                for b in range(2):
                    own = pl.ds(b * half, half)
                    w = nn(low[h % group, own, own] * masks[level], tb[h, b]).astype(BF)
                    tb[h, b] = tb[h, b] - nn(tb[h, b], w).astype(BF)
        for h in hs:
            w = nn(low[h % group, half:, :half], tb[h, 0]).astype(BF)
            cross_part = nn(tb[h, 1], w)
            tb[h] = jnp.concatenate([
                jnp.concatenate([tb[h, 0], jnp.zeros((half, half), BF)], 1),
                jnp.concatenate([(-cross_part).astype(BF), tb[h, 1]], 1),
            ], 0)
        for h in hs:
            gq, vb, kbg, tk, end = keep[h]
            t_ref[h] = tb[h]
            m = nn(score[h], tb[h])
            mb = m.astype(BF)
            m_ref[h] = mb
            mix = nn(tb[h], jnp.concatenate([vb, kbg], 1)).astype(BF)
            nk_ref[h] = mix
            au = tn(mix, tk)
            r2, l2 = iotas(128, 128)
            au_ref[h, 0:128] = au[0:128].astype(BF)
            au_ref[h, 128:256] = (jnp.where(r2 == l2, jnp.exp(end), 0.0) - au[128:256]).astype(BF)
            lam = jnp.where(cross < 64, col(lam_all, lane_of(h, 0, heads)),
                            jnp.where(cross < 128, col(lam_all, lane_of(h, 1, heads)), col(lam_all, lane_of(h, 2, heads))))
            core_ref[h] = nn((m * lam).astype(BF), vb)
            qh_ref[h] = (gq - nn(mb, kbg)).astype(BF)


def local_forward(head_param, proj, gate, levels):
    rows = proj.shape[0]
    heads = head_param.shape[1]
    group = 4
    square = jax.ShapeDtypeStruct((heads, rows, rows), BF)
    bits = rows.bit_length() - 1
    return pl.pallas_call(
        functools.partial(local_kernel, heads, levels, group),
        in_specs=[pl.BlockSpec(memory_space=pltpu.SMEM), pl.BlockSpec(memory_space=VM), pl.BlockSpec(memory_space=VM)],
        out_specs=[pl.BlockSpec(memory_space=VM)] * 9,
        out_shape=[
            jax.ShapeDtypeStruct((heads, 256, 128), BF),
            square, square, square, square,
            jax.ShapeDtypeStruct((heads, rows, 256), BF),
            jax.ShapeDtypeStruct((heads, rows, 128), F32),
            jax.ShapeDtypeStruct((heads, rows, 128), BF),
            jax.ShapeDtypeStruct((rows, heads * LANES), F32),
        ],
        scratch_shapes=[VM((bits - 1, rows // 2, rows // 2), BF), VM((group, rows, rows), BF)],
        compiler_params=pltpu.CompilerParams(vmem_limit_bytes=LIMIT["local"] * 2**20),
        name="local_forward",
    )(head_param, proj, gate)


def out_kernel(heads, levels, far, near, gate_ref, core_ref, qh_ref, x_ref, gain_ref, gn_ref,
               normed_ref, g_ref, dqh_ref, gx_ref, dlam_ref):
    n = gate_ref.shape[0]
    lam_all = softplus(gate_ref[...])
    lane = lax.broadcasted_iota(jnp.int32, (n, heads * LANES), 1)
    gain = gain_ref[...]
    dlam = jnp.zeros((n, heads * LANES), F32)
    for h in range(heads):
        qh = qh_ref[h]
        x = x_ref[h]
        w = nt(qh, x)
        core = core_ref[h]
        fw = [col(lam_all, lane_of(h, near + j, heads)) for j in range(far)]
        for j in range(far):
            core = core + fw[j] * w[:, j * 128 : (j + 1) * 128]
        rs = lax.rsqrt(jnp.mean(core * core, -1, keepdims=True) + 1e-06)
        unit_core = core * rs
        normed_ref[:, h * 128 : (h + 1) * 128] = (unit_core * gain).astype(BF)
        gy = gn_ref[:, h * 128 : (h + 1) * 128] * gain
        g = rs * (gy - unit_core * jnp.mean(gy * unit_core, -1, keepdims=True))
        g_ref[h] = g.astype(BF)
        fg = jnp.concatenate([(fw[j] * g).astype(BF) for j in range(far)], 1)
        for j in range(far):
            here = jnp.sum(g * w[:, j * 128 : (j + 1) * 128], -1, keepdims=True)
            dlam = jnp.where(lane == lane_of(h, near + j, heads), here, dlam)
        dqh_ref[h] = nn(fg, x).astype(BF)
        gx_ref[h] = tn(fg, qh).astype(BF)
    dlam_ref[...] = dlam


def out_stage(gate, core, qh, x, gain, grad_normed, levels, far, near):
    rows = gate.shape[0]
    heads = core.shape[0]
    return pl.pallas_call(
        functools.partial(out_kernel, heads, levels, far, near),
        in_specs=[pl.BlockSpec(memory_space=VM)] * 6,
        out_specs=[pl.BlockSpec(memory_space=VM)] * 5,
        out_shape=[
            jax.ShapeDtypeStruct((rows, heads * 128), BF),
            jax.ShapeDtypeStruct((heads, rows, 128), BF),
            jax.ShapeDtypeStruct((heads, rows, 128), BF),
            jax.ShapeDtypeStruct((heads, far * 128, 128), BF),
            jax.ShapeDtypeStruct((rows, heads * LANES), F32),
        ],
        compiler_params=pltpu.CompilerParams(vmem_limit_bytes=LIMIT["out"] * 2**20),
        name="out_stage",
    )(gate, core, qh, x, gain, grad_normed)


def back_kernel(heads, levels, group, param_ref, proj_ref, gate_ref, clog_ref, e_ref, lp_ref, t_ref, m_ref,
                nk_ref, g_ref, dqh_ref, dau_ref, dlam_ref, layer_ref, dproj_ref, dgate_ref, out_ref):
    n = proj_ref.shape[0]
    gate = gate_ref[...]
    rate, bias = head_rows(param_ref, heads, n)
    clog = clog_ref[...]
    beta_all = sigmoid(gate + bias)
    sig_all = sigmoid(gate)
    lam_all = softplus(gate)
    row, lane = iotas(n, n)
    cross = jnp.bitwise_xor(row, lane)
    strict = row > lane
    eye = jnp.where(row == lane, 1.0, 0.0).astype(BF)

    def tq(a, b):
        return nn(nt(eye, a).astype(BF), b)

    out_ref[...] = layer_ref[...]
    wide = lax.broadcasted_iota(jnp.int32, (n, heads * LANES), 1)
    dlam = dlam_ref[...]
    source, target = iotas(n, heads * LANES)

    def pick_level(block, h):
        apart = jnp.bitwise_xor(jnp.right_shift(source, 6), block)
        near_level = jnp.where(apart == 0, 0, jnp.where(apart == 1, 1, 2))
        return jnp.where(target == near_level * heads + h, 1.0, 0.0).astype(BF)

    dlog = jnp.zeros((n, heads * LANES), F32)
    dbeta_all = jnp.zeros((n, heads * LANES), F32)
    last = lax.broadcasted_iota(jnp.int32, (n, 1), 0) == n - 1
    out = [None] * (3 * heads)
    for first in range(0, heads, group):
        for h in range(first, first + group):
            q, rq = unit(proj_ref[:, h * 128 : (h + 1) * 128])
            k, rk = unit(proj_ref[:, (heads + h) * 128 : (heads + h + 1) * 128])
            v = proj_ref[:, (2 * heads + h) * 128 : (2 * heads + h + 1) * 128]
            qb, kb = q.astype(BF), k.astype(BF)
            beta = col(beta_all, lane_of(h, levels + 1, heads))
            cc = col(clog, lane_of(h, levels, heads))
            at = lane_of(h, levels, heads)
            end = clog[n - 1 : n, at : at + 1]
            grow = jnp.exp(cc)
            tail = jnp.exp(end - cc)
            vb = (v * beta).astype(BF)
            kbg = ((beta * grow) * k).astype(BF)
            tk = (tail * k).astype(BF)
            g, dqh = g_ref[h], dqh_ref[h]
            mb, tb, mix = m_ref[h], t_ref[h], nk_ref[h]
            m = mb.astype(F32)
            lam = jnp.where(cross < 64, col(lam_all, lane_of(h, 0, heads)),
                            jnp.where(cross < 128, col(lam_all, lane_of(h, 1, heads)), col(lam_all, lane_of(h, 2, heads))))
            dmw = nt(g, vb)
            prod = m * dmw
            pb = prod.astype(BF)
            dlam = dlam + jnp.concatenate(
                [nn(pb[b * 64 : (b + 1) * 64], pick_level(b, h)) for b in range(n // 64)], 0)
            mw = (m * lam).astype(BF)
            dm = (lam * dmw - nt(dqh, kbg)).astype(BF)
            dau = dau_ref[h]
            du, da = dau[0:128], dau[128:256]
            dnv = nt(tk, du)
            dkt = -nt(tk, da)
            dtk = nn(mix[:, 0:128], du) - nn(mix[:, 128:256], da)
            dmix = jnp.concatenate([dnv.astype(BF), dkt.astype(BF)], 1)
            back = tq(tb, dmix)
            dvb2, dkbg2 = back[:, 0:128], back[:, 128:256]
            dst = nt(dm, tb)
            dstb = dst.astype(BF)
            dvb = tq(mw, g) + dvb2
            both = tq(mb, jnp.concatenate([dqh, dstb], 1))
            dkbg = dkbg2 - both[:, 0:128]
            dlow = both[:, 128:] + nt(back.astype(BF), mix)
            dlow = jnp.where(strict, -dlow, 0.0)
            e = e_ref[h].astype(F32)
            dp = (dst * e).astype(BF)
            lp = lp_ref[h].astype(F32)
            dbeta = jnp.sum(dlow * lp, -1, keepdims=True)
            dkk = (dlow * (beta * e)).astype(BF)
            dq1 = nn(dp, kb)
            dk1 = tq(dp, qb)
            dk2 = nn(dkk, kb)
            dk3 = tq(dkk, kb)
            qr, kr = qb.astype(F32), kb.astype(F32)
            dqf, dtf, dkf = dqh.astype(F32), dtk, dkbg
            gq = jnp.sum(dqf * q, -1, keepdims=True)
            kk = jnp.sum(dkf * k, -1, keepdims=True)
            dtail = jnp.sum(dtf * k, -1, keepdims=True) * tail
            dc = jnp.sum(qr * dq1 + kr * (dk2 - dk1 - dk3), -1, keepdims=True)
            dc = dc + grow * (gq + beta * kk) - dtail
            r2, l2 = iotas(128, 128)
            trace = jnp.sum(jnp.where(r2 == l2, da.astype(F32), 0.0), keepdims=True)
            dend = jnp.sum(dtail, keepdims=True) + jnp.exp(end) * trace
            dc = dc + jnp.where(last, dend, 0.0)
            dbeta = dbeta + jnp.sum(dvb * v, -1, keepdims=True) + grow * kk
            dq = dq1 + grow * dqf
            dk = dk1 + dk2 + dk3 + (beta * grow) * dkf + tail * dtf
            dv = beta * dvb
            out[h] = (rq * (dq - q * jnp.sum(q * dq, -1, keepdims=True))).astype(BF)
            out[heads + h] = (rk * (dk - k * jnp.sum(k * dk, -1, keepdims=True))).astype(BF)
            out[2 * heads + h] = dv.astype(BF)
            dlog = jnp.where(wide == lane_of(h, levels, heads), dc, dlog)
            dbeta_all = jnp.where(wide == lane_of(h, levels + 1, heads), dbeta, dbeta_all)
    upper = jnp.where(lane >= row, 1.0, 0.0).astype(F32)
    dstep = lax.dot_general(upper, dlog, (((1,), (0,)), ((), ())),
                            precision=lax.Precision.HIGHEST, preferred_element_type=F32)
    dgate = dlam * sig_all - rate * sig_all * (1.0 - sig_all) * dstep + beta_all * (1.0 - beta_all) * dbeta_all
    dgate_ref[...] = dgate.astype(BF)
    for j, grad in enumerate(out):
        dproj_ref[:, j * 128 : (j + 1) * 128] = grad


def back_stage(head_param, proj, gate, clog, saved, g, dqh, dau, dlam, layer, levels):
    rows = proj.shape[0]
    heads = head_param.shape[1]
    return pl.pallas_call(
        functools.partial(back_kernel, heads, levels, 1),
        in_specs=[pl.BlockSpec(memory_space=pltpu.SMEM)] + [pl.BlockSpec(memory_space=VM)] * 13,
        out_specs=[pl.BlockSpec(memory_space=VM)] * 3,
        out_shape=[jax.ShapeDtypeStruct((rows, 3 * heads * 128), BF), jax.ShapeDtypeStruct((rows, heads * LANES), BF),
                   jax.ShapeDtypeStruct(layer.shape, BF)],
        compiler_params=pltpu.CompilerParams(vmem_limit_bytes=LIMIT["back"] * 2**20),
        name="back_stage",
    )(head_param, proj, gate, clog, *saved, g, dqh, dau, dlam, layer)


MESH = pl.DeviceIdType.MESH
RING = 4


def place():
    ctx = lax.axis_index("ctx")
    return lax.div(ctx, 2 * RING), lax.rem(lax.div(ctx, 2), RING), lax.rem(ctx, 2)


def at_ctx(x, y, core):
    return {"ctx": (x * RING + y) * 2 + core}


def around(index, step):
    return lax.rem(index + step + RING, RING)


def greet(peers, meanwhile):
    barrier = pltpu.get_barrier_semaphore()
    for peer in peers:
        pl.semaphore_signal(barrier, inc=1, device_id=peer, device_id_type=MESH)
    meanwhile()
    pl.semaphore_wait(barrier, len(peers))


def remote(src, dst, send, recv, index, peer):
    return pltpu.make_async_remote_copy(
        src_ref=src, dst_ref=dst, send_sem=send.at[index], recv_sem=recv.at[index],
        device_id=peer, device_id_type=MESH)


class Ring:
    def __init__(self, buf, i, send, recv, base, right, left, low, middle):
        rows = buf.shape[2]
        first, second, whole = pl.ds(low, middle - low), pl.ds(middle, rows - middle), pl.ds(0, middle)

        def copy(index, slot, to, part, peer):
            return remote(buf.at[slot, i, part], buf.at[to, i, part], send, recv, base + index, peer)

        self.near = [copy(0, 0, 1, first, right), copy(1, 0, 3, second, left),
                     copy(2, 0, 1, second, right), copy(3, 0, 3, whole, left)]
        self.far = [copy(4, 1, 2, first, right), copy(5, 3, 2, second, left)]
        for one in self.near:
            one.start()

    def relay(self):
        for near, far in zip(self.near, self.far):
            near.wait_recv()
            far.start()

    def arrive(self):
        for one in self.near[2:] + self.far:
            one.wait_recv()

    def leave(self):
        for one in self.near + self.far:
            one.wait_send()


def flag(cond):
    return jnp.where(cond, 1.0, 0.0).astype(F32)


def gather_kernel(au_ref, gout_ref, ow_ref, x_ref, cores_ref, ys_ref, xs_ref, gn_ref, cores, ys, xs, share, send, recv, local):
    x, y, core = place()
    partner = at_ctx(x, y, 1 - core)
    y_right, y_left = at_ctx(x, around(y, 1), core), at_ctx(x, around(y, -1), core)
    x_right, x_left = at_ctx(around(x, 1), y, core), at_ctx(around(x, -1), y, core)

    def product():
        gn_ref[...] = nt(gout_ref[...], ow_ref[...])

    greet((partner, y_right, y_left, x_right, x_left), product)
    first = core * 2
    mine, yours = pl.ds(first, 2), pl.ds(2 - first, 2)
    out = [remote(au_ref.at[part], cores.at[core, part], send, recv, k, partner) for k, part in enumerate((yours, mine))]
    take = [remote(au_ref.at[part], cores.at[1 - core, part], send, recv, k, partner) for k, part in enumerate((mine, yours))]
    for one in out:
        one.start()
    keep = pltpu.make_async_copy(au_ref, cores.at[core], local.at[0])
    keep.start()
    eye_r, eye_c = iotas(128, 128)
    eye = jnp.where(eye_r == eye_c, 1.0, 0.0).astype(F32)

    def joined(below, above):
        moved = nn(below, above[128:256])
        return jnp.concatenate([moved[0:128] + above[0:128].astype(F32), moved[128:256]], 0)

    keep.wait()
    take[0].wait_recv()
    ring = []
    for i in range(2):
        ys[0, i] = joined(cores[0, first + i], cores[1, first + i]).astype(BF)
        ring.append(Ring(ys, i, send, recv, 2 + 6 * i, y_right, y_left, 0, 128))
    for i in range(2):
        ring[i].relay()
    prefix = [None, None]
    cols = []
    for i in range(2):
        ring[i].arrive()
        at = [ys[around(y, -k), i] for k in range(RING)]
        s1 = joined(at[0], at[1])
        s2 = joined(s1.astype(BF), at[2])
        s3 = joined(s2.astype(BF), at[3])
        xs[0, i] = s3.astype(BF)
        cols.append(Ring(xs, i, send, recv, 14 + 6 * i, x_right, x_left, 0, 128))
        x1 = flag(lax.rem(y, 2) == 1) * ys[1, i, 0:128].astype(F32)
        s1u = s1[0:128]
        x2 = flag(y == 2) * s1u + flag(y == 3) * nn(s1u.astype(BF), at[2][128:256])
        share[first + i, 0:128] = x1.astype(BF)
        share[first + i, 128:256] = x2.astype(BF)
        prefix[i] = (flag(y == 0) * eye + flag(y == 1) * at[0][128:256].astype(F32)
                     + flag(y == 2) * s1[128:256] + flag(y == 3) * s2[128:256]).astype(BF)
    for i in range(2):
        cols[i].relay()
    give, got = [], []
    for i in range(2):
        cols[i].arrive()
        at = [xs[around(x, -k), i] for k in range(RING)]
        r1 = nn(at[0][0:128], at[1][128:256]) + at[1][0:128].astype(F32)
        x3 = flag(lax.rem(x, 2) == 1) * xs[1, i, 0:128].astype(F32)
        x4 = flag(x == 2) * r1 + flag(x == 3) * nn(r1.astype(BF), at[2][128:256])
        both = jnp.concatenate([x3.astype(BF), x4.astype(BF)], 0)
        share[first + i, 256:512] = nn(both, prefix[i]).astype(BF)
        give.append(remote(share.at[first + i], share.at[first + i], send, recv, 26 + i, partner))
        got.append(remote(share.at[2 - first + i], share.at[2 - first + i], send, recv, 26 + i, partner))
        give[i].start()
    upper = flag(core == 1)
    take[1].wait_recv()
    step = []
    for h in range(4):
        below = cores[0, h]
        x_ref[h, 0:128] = (upper * below[0:128].astype(F32)).astype(BF)
        step.append((upper * below[128:256].astype(F32) + (1.0 - upper) * eye).astype(BF))
    cores_ref[...] = cores[...]
    ys_ref[...] = ys[...]
    xs_ref[...] = xs[...]
    for i in range(2):
        x_ref[first + i, 128:640] = nn(share[first + i], jnp.where(core == 0, step[i], step[2 + i])).astype(BF)
    for i in range(2):
        got[i].wait_recv()
        x_ref[2 - first + i, 128:640] = nn(share[2 - first + i], jnp.where(core == 0, step[2 + i], step[i])).astype(BF)
    for one in out + give:
        one.wait_send()
    for one in ring + cols:
        one.leave()


def gather_states(au, grad_out, out_weight):
    heads = au.shape[0]
    cores = ((2, heads, 256, 128), BF)
    ring = ((RING, 2, 256, 128), BF)
    return pl.pallas_call(
        gather_kernel,
        in_specs=[pl.BlockSpec(memory_space=VM)] * 3,
        out_specs=[pl.BlockSpec(memory_space=VM)] * 5,
        out_shape=[jax.ShapeDtypeStruct((heads, 640, 128), BF)] + [jax.ShapeDtypeStruct(*s) for s in (cores, ring, ring)]
        + [jax.ShapeDtypeStruct((grad_out.shape[0], heads * 128), F32)],
        scratch_shapes=[VM(*cores), VM(*ring), VM(*ring), VM((heads, 512, 128), BF),
                        pltpu.SemaphoreType.DMA((28,)), pltpu.SemaphoreType.DMA((28,)), pltpu.SemaphoreType.DMA((1,))],
        compiler_params=pltpu.CompilerParams(
            collective_id=1, has_side_effects=True, vmem_limit_bytes=LIMIT["gather"] * 2**20),
        name="gather_states",
    )(au, grad_out, out_weight)


def return_kernel(groups, gx_ref, x_ref, cores_ref, ys_ref, xs_ref, normed_ref, ow_ref, dau_ref, layer_ref,
                  part_ref, pair, ys, xs, share, chunks, send, recv, local, zsend, zrecv):
    x, y, core = place()
    z = lax.axis_index("head")
    partner = at_ctx(x, y, 1 - core)
    y_right, y_left = at_ctx(x, around(y, 1), core), at_ctx(x, around(y, -1), core)
    x_right, x_left = at_ctx(around(x, 1), y, core), at_ctx(around(x, -1), y, core)
    across = [{"head": lax.rem(z + k, groups)} for k in range(1, groups)]
    wide = part_ref.shape[2]

    def product():
        for j in range(groups):
            part_ref[j] = nn(normed_ref[...], ow_ref[:, j * wide : (j + 1) * wide]).astype(BF)

    greet([partner, y_right, y_left, x_right, x_left] + across, product)
    first = core * 2
    mine, yours = pl.ds(first, 2), pl.ds(2 - first, 2)
    out = [remote(gx_ref.at[part], pair.at[core, part], send, recv, k, partner) for k, part in enumerate((yours, mine))]
    take = [remote(gx_ref.at[part], pair.at[1 - core, part], send, recv, k, partner) for k, part in enumerate((mine, yours))]
    for one in out:
        one.start()
    keep = pltpu.make_async_copy(gx_ref, pair.at[core], local.at[0])
    keep.start()
    spread = []
    for k in range(1, groups):
        to = lax.rem(z + k, groups)
        spread.append(remote(part_ref.at[to], chunks.at[k - 1], zsend, zrecv, k - 1, across[k - 1]))
        spread[-1].start()
    upper = flag(core == 1)
    bits = [upper, flag(lax.rem(y, 2) == 1), flag(y >= 2), flag(lax.rem(x, 2) == 1), flag(x >= 2)]
    eye_r, eye_c = iotas(128, 128)
    eye = jnp.where(eye_r == eye_c, 1.0, 0.0).astype(F32)
    after = [None, None]
    for i in range(2):
        at = [ys_ref[around(y, -k), i, 128:256] for k in range(RING)]
        q1 = nn(at[2], at[3])
        q0 = nn(at[1], q1.astype(BF))
        after[i] = (flag(y == 3) * eye + flag(y == 2) * at[3].astype(F32) + flag(y == 1) * q1 + flag(y == 0) * q0).astype(BF)
    keep.wait()
    take[0].wait_recv()
    ring = []
    for i in range(2):
        total = pair[0, first + i, 128:640].astype(F32) + nt(pair[1, first + i, 128:640], cores_ref[0, first + i, 128:256])
        for k in range(4):
            ys[0, i, k * 128 : (k + 1) * 128] = (bits[k + 1] * total[k * 128 : (k + 1) * 128]).astype(BF)
        ring.append(Ring(ys, i, send, recv, 2 + 6 * i, y_right, y_left, 128, 384))
    for i in range(2):
        ring[i].relay()
    held = [None, None]
    cols = []
    for i in range(2):
        ring[i].arrive()
        trans = [ys_ref[around(y, -k), i, 128:256] for k in range(RING)]
        at = [ys[around(y, -k), i, 128:512] for k in range(RING)]
        h1 = nt(at[3], trans[2]) + at[2].astype(F32)
        h0 = nt(h1.astype(BF), trans[1]) + at[1].astype(F32)
        column = nt(h0[128:384].astype(BF), trans[0]) + at[0][128:384].astype(F32)
        xs[0, i] = column.astype(BF)
        cols.append(Ring(xs, i, send, recv, 14 + 6 * i, x_right, x_left, 0, 128))
        held[i] = flag(y == 2) * at[3].astype(F32) + flag(y == 1) * h1 + flag(y == 0) * h0
        share[first + i, 0:128] = ((1.0 - bits[1]) * ys[3, i, 0:128].astype(F32)).astype(BF)
        share[first + i, 128:256] = held[i][0:128].astype(BF)
    for i in range(2):
        cols[i].relay()
    give, got = [], []
    for i in range(2):
        cols[i].arrive()
        trans = [xs_ref[around(x, -k), i, 128:256] for k in range(RING)]
        at = [xs[around(x, -k), i, 128:256] for k in range(RING)]
        h1 = nt(at[3], trans[2]) + at[2].astype(F32)
        h0 = nt(h1.astype(BF), trans[1]) + at[1].astype(F32)
        v4 = flag(x == 2) * at[3].astype(F32) + flag(x == 1) * h1 + flag(x == 0) * h0
        v3 = (1.0 - bits[3]) * xs[3, i, 0:128].astype(F32)
        both = jnp.concatenate([v3.astype(BF), v4.astype(BF)], 0)
        share[first + i, 256:512] = (held[i][128:384] + nt(both, after[i])).astype(BF)
        give.append(remote(share.at[first + i], share.at[first + i], send, recv, 26 + i, partner))
        got.append(remote(share.at[2 - first + i], share.at[2 - first + i], send, recv, 26 + i, partner))
        give[i].start()
    take[1].wait_recv()

    def finish(h):
        move = (upper * eye + (1.0 - upper) * cores_ref[1, h, 128:256].astype(F32)).astype(BF)
        v = nt(share[h], move)
        parts = [(1.0 - upper) * pair[1, h, 0:128].astype(F32)]
        for k in range(4):
            keep_it = (1.0 - upper) * bits[k + 1]
            parts.append(v[k * 128 : (k + 1) * 128] + keep_it * pair[1, h, (k + 1) * 128 : (k + 2) * 128].astype(F32))
        so_far = jnp.zeros((128, 128), F32)
        du = jnp.zeros((128, 128), F32)
        states = []
        for k in range(5):
            state = x_ref[h, k * 128 : (k + 1) * 128].astype(F32)
            states.append((bits[k] * state + (1.0 - bits[k]) * so_far).astype(BF))
            so_far = so_far + state
            du = du + (1.0 - bits[k]) * parts[k]
        da = tn(jnp.concatenate(states, 0), jnp.concatenate([p.astype(BF) for p in parts], 0))
        dau_ref[h, 0:128] = du.astype(BF)
        dau_ref[h, 128:256] = da.astype(BF)

    for i in range(2):
        finish(first + i)
    total = part_ref[z].astype(F32)
    for copy in spread:
        copy.wait_recv()
    for k in range(groups - 1):
        total = total + chunks[k].astype(F32)
    layer_ref[...] = total.astype(BF)
    for i in range(2):
        got[i].wait_recv()
        finish(2 - first + i)
    for one in out + give + spread:
        one.wait_send()
    for one in ring + cols:
        one.leave()


def return_grads(gx, x, cores, ys, xs, normed, out_weight, groups):
    heads = gx.shape[0]
    rows, wide = normed.shape[0], out_weight.shape[1] // groups
    ring = (RING, 2)
    return pl.pallas_call(
        functools.partial(return_kernel, groups),
        in_specs=[pl.BlockSpec(memory_space=VM)] * 7,
        out_specs=[pl.BlockSpec(memory_space=VM)] * 2,
        out_shape=[jax.ShapeDtypeStruct((heads, 256, 128), BF), jax.ShapeDtypeStruct((rows, wide), BF)],
        scratch_shapes=[VM((groups, rows, wide), BF), VM((2, heads, 640, 128), BF), VM(ring + (512, 128), BF), VM(ring + (256, 128), BF),
                        VM((heads, 512, 128), BF), VM((3, rows, wide), BF),
                        pltpu.SemaphoreType.DMA((28,)), pltpu.SemaphoreType.DMA((28,)), pltpu.SemaphoreType.DMA((1,)),
                        pltpu.SemaphoreType.DMA((3,)), pltpu.SemaphoreType.DMA((3,))],
        compiler_params=pltpu.CompilerParams(
            collective_id=2, has_side_effects=True, vmem_limit_bytes=LIMIT["return"] * 2**20),
        name="return_grads",
    )(gx, x, cores, ys, xs, normed, out_weight)


def last_kernel(groups, dproj_ref, dgate_ref, w_ref, sw_ref, out_ref, mine, relay, direct, extra, arrive, send, recv):
    rows, wide = out_ref.shape
    z = lax.axis_index("head")
    half = wide // 2
    right, left = {"head": lax.rem(z + 1, groups)}, {"head": lax.rem(z + groups - 1, groups)}
    dproj, dgate = dproj_ref[...], dgate_ref[...]

    def product(step):
        chunk = lax.rem(z + step + groups, groups)
        at = pl.ds(pl.multiple_of(chunk * wide, wide), wide)
        return nt(dproj, w_ref[at, :]) + nn(dgate, sw_ref[:, at])

    def farthest():
        far = product(2)
        relay[0] = far[:, :half].astype(BF)
        relay[1] = far[:, half:].astype(BF)

    greet((right, left), farthest)
    far_right = remote(relay.at[0], arrive.at[0], send, recv, 0, right)
    far_left = remote(relay.at[1], arrive.at[1], send, recv, 1, left)
    far_right.start()
    far_left.start()
    to_right = product(1)
    direct[0] = to_right[:, half:].astype(BF)
    near_right = remote(direct.at[0], arrive.at[2], send, recv, 2, right)
    near_right.start()
    to_left = product(-1)
    direct[1] = to_left[:, :half].astype(BF)
    near_left = remote(direct.at[1], arrive.at[3], send, recv, 3, left)
    near_left.start()
    far_right.wait_recv()
    extra[0] = (to_right[:, :half] + arrive[0].astype(F32)).astype(BF)
    sum_right = remote(extra.at[0], arrive.at[4], send, recv, 4, right)
    sum_right.start()
    far_left.wait_recv()
    extra[1] = (to_left[:, half:] + arrive[1].astype(F32)).astype(BF)
    sum_left = remote(extra.at[1], arrive.at[5], send, recv, 5, left)
    sum_left.start()
    mine[...] = product(0)
    near_right.wait_recv()
    near_left.wait_recv()
    sum_right.wait_recv()
    sum_left.wait_recv()
    out_ref[:, :half] = (mine[:, :half] + arrive[4].astype(F32) + arrive[3].astype(F32)).astype(BF)
    out_ref[:, half:] = (mine[:, half:] + arrive[5].astype(F32) + arrive[2].astype(F32)).astype(BF)
    for copy in (far_right, far_left, near_right, near_left, sum_right, sum_left):
        copy.wait_send()


def last_stage(dproj, dgate, wflat, swt, groups):
    rows = dproj.shape[0]
    wide = wflat.shape[0] // groups
    half = (rows, wide // 2)
    return pl.pallas_call(
        functools.partial(last_kernel, groups),
        in_specs=[pl.BlockSpec(memory_space=VM)] * 4,
        out_specs=pl.BlockSpec(memory_space=VM),
        out_shape=jax.ShapeDtypeStruct((rows, wide), BF),
        scratch_shapes=[VM((rows, wide), F32), VM((2,) + half, BF), VM((2,) + half, BF), VM((2,) + half, BF),
                        VM((6,) + half, BF), pltpu.SemaphoreType.DMA((6,)), pltpu.SemaphoreType.DMA((6,))],
        compiler_params=pltpu.CompilerParams(
            collective_id=3, has_side_effects=True, vmem_limit_bytes=LIMIT["last"] * 2**20),
        name="last_stage",
    )(dproj, dgate, wflat, swt)


def on_device(tokens, qkv_weight, small_weight, head_param, norm_gain, out_weight, grad_out):
    rows, width = tokens.shape
    heads = qkv_weight.shape[2]
    levels = small_weight.shape[2] - 2
    near = (rows // 64).bit_length()
    far = lax.axis_size("ctx").bit_length() - 1
    groups = lax.axis_size("head")
    rates = head_param.T
    proj, gate, wflat, swt = project(tokens, qkv_weight, small_weight)
    au, *saved, core, qh, clog = local_forward(rates, proj, gate, levels)
    flat_out = out_weight.reshape(heads * 128, width)
    x, cores, ys, xs, grad_normed = gather_states(au, grad_out, flat_out)
    normed, g, dqh, gx, dlam = out_stage(gate, core, qh, x, norm_gain.reshape(1, -1), grad_normed, levels, far, near)
    dau, layer = return_grads(gx, x, cores, ys, xs, normed, flat_out, groups)
    dproj, dgate, layer_out = back_stage(rates, proj, gate, clog, saved, g, dqh, dau, dlam, layer, levels)
    grad_tokens = last_stage(dproj, dgate, wflat, swt, groups)
    return (layer_out, grad_tokens)


def solution(mesh):
    placed = (
        P("ctx", None),
        P(None, None, "head", None),
        P(None, "head", None),
        P("head", None),
        P(),
        P("head", None, None),
        P("ctx", None),
    )
    return jax.shard_map(
        on_device,
        mesh=mesh,
        in_specs=placed,
        out_specs=(P("ctx", "head"), P("ctx", "head")),
        check_vma=False,
    )
```
